32 devices in a mesh: dp: 8 (over y, x, core), tensor: 4 (over z).
Axes of the slice: x: 2, y: 2, z: 4, core: 2. Of those that a mesh axis runs over, the one named last changes fastest.
Arguments:
- hidden_in: bfloat16 [8, 512, 2048], P(None, 'dp'), may hold values from -6 to 6
- layer_inputs: bfloat16 [8, 512, 256], P(None, 'dp'), may hold values from -6 to 6
- out_grad: bfloat16 [8, 512, 2048], P(None, 'dp'), may hold values from -6 to 6
- lengths: int32 [3], replicated, may hold values from 1024 to 2048, as said below
- order: int32 [3], replicated, may hold values from 0 to 2, each once
- w_query: bfloat16 [2048, 2048], P('dp', 'tensor'), may hold values from -0.125 to 0.125
- w_keyval: bfloat16 [2, 2048, 512], P(None, 'dp'), may hold values from -0.125 to 0.125
- w_out: bfloat16 [2048, 2048], P('tensor', 'dp'), may hold values from -0.125 to 0.125
- w_left: bfloat16 [2048, 64], P('dp'), may hold values from -0.125 to 0.125
- w_right: bfloat16 [64, 2048], P(None, 'dp'), may hold values from -0.75 to 0.75
- w_gateup: bfloat16 [2, 2048, 8192], P(None, 'dp', 'tensor'), may hold values from -0.125 to 0.125
- w_down: bfloat16 [8192, 2048], P('tensor', 'dp'), may hold values from -0.0625 to 0.0625
- w_pergate: bfloat16 [2048, 256], P('dp'), may hold values from -0.125 to 0.125
- w_perproj: bfloat16 [256, 2048], P(None, 'dp'), may hold values from -0.375 to 0.375
- gains: float32 [6, 2048], P(None, 'dp'), may hold values from 0.5 to 1.5
- head_gains: float32 [2, 256], replicated, may hold values from 0.25 to 0.45
Outputs:
- output: bfloat16 [8, 512, 2048], P(None, 'dp')
- input_grad: bfloat16 [8, 512, 2048], P(None, 'dp')
- layer_grad: bfloat16 [8, 512, 256], P(None, 'dp')
- grad_query: float32 [2048, 2048], P('dp', 'tensor')
- grad_keyval: float32 [2, 2048, 512], P(None, 'dp')
- grad_out: float32 [2048, 2048], P('tensor', 'dp')
- grad_left: float32 [2048, 64], P('dp')
- grad_right: float32 [64, 2048], P(None, 'dp')
- grad_gateup: float32 [2, 2048, 8192], P(None, 'dp', 'tensor')
- grad_down: float32 [8192, 2048], P('tensor', 'dp')
- grad_pergate: float32 [2048, 256], P('dp')
- grad_perproj: float32 [256, 2048], P(None, 'dp')
- grad_gains: float32 [6, 2048], P(None, 'dp')
- grad_head_gains: float32 [2, 256], replicated
The draws below stay inside these ranges and needn't reach their ends.
Inputs may be any that keep to these rules, and one draw needn't show every extreme that they name: 3 lengths of 1024 to 2048 tokens that sum to 4096; one is 2048. `order`: each of 0 to 2 once.
All inputs are finite; a program needn't handle non-finite values.
Results may differ from the reference program's by a relative error of at most 0.04.
Values may be sent and summed in bfloat16 or wider, within the bound.
No kernel may reach another device: no remote copies, remote signals or barrier semaphores. Data moves between devices by JAX's collectives and lax.ppermute only.
A program may use at most 256 MiB of HBM per device.

```python
import jax
import jax.numpy as jnp
from jax import lax

D = 2048
QH = 8
KVH = 2
HD = 256
FF = 8192
LRANK = 64
PLDIM = 256
WIN = 512
LMIN = 1024
LMAX = 2048
TOKENS = 4096
MICRO = 8
STRETCH = 512
SEQS = 3
N_TENSOR = 4


def draw_lengths(key, part):
    extra_total = TOKENS - SEQS * LMIN
    top_extra = LMAX - LMIN
    rest_total = extra_total - top_extra
    others = SEQS - 2
    base_share = rest_total // others
    remainder = rest_total - base_share * others
    jitter = max(1, min(base_share, top_extra - base_share))
    key_one, key_two, key_three = jax.random.split(key, 3)
    offsets = jax.random.randint(key_one, (others,), 0, jitter).astype(jnp.int32)
    shares = base_share + offsets - jnp.roll(offsets, 1) + (jnp.arange(others) < remainder).astype(jnp.int32)
    longest = jax.random.randint(key_two, (), 0, SEQS)
    shortest = (longest + 1 + jax.random.randint(key_three, (), 0, SEQS - 1)) % SEQS
    seq_ids = jnp.arange(SEQS)
    other_rank = seq_ids - (seq_ids > longest).astype(jnp.int32) - (seq_ids > shortest).astype(jnp.int32)
    picked = jnp.take(shares, jnp.clip(other_rank, 0, others - 1))
    extra = jnp.where(seq_ids == longest, top_extra, jnp.where(seq_ids == shortest, 0, picked))
    return (LMIN + extra).astype(jnp.int32)


def levels(key, dims, pieces, least, top_value):
    factor_of = 1.0
    for position, parts in pieces:
        draws = jax.random.uniform(jax.random.fold_in(jax.random.fold_in(key, 6), position), (parts,), jnp.float32, least / len(pieces), top_value / len(pieces))
        factor_of = factor_of * jnp.repeat(jnp.exp(draws), dims[position] // parts).reshape((-1,) + (1,) * (len(dims) - 1 - position))
    return factor_of


def centred(stream_key, dims, spread, bound, cuts=(), kind=jnp.bfloat16):
    values = spread * jax.random.normal(stream_key, dims, jnp.float32)
    if cuts:
        values = values * levels(stream_key, dims, cuts, -0.22, 0.18)
    return jnp.clip(values, -bound, bound).astype(kind)


def setup_inputs(seed: int = 0) -> dict:
    splits = jax.random.split(jax.random.key(seed), 17)
    hidden_in = centred(splits[0], (MICRO, STRETCH, D), 1.0, 6.0, ((1, 8),))
    layer_inputs = centred(splits[1], (MICRO, STRETCH, PLDIM), 1.0, 6.0, ((1, 8),))
    out_grad = centred(splits[2], (MICRO, STRETCH, D), 1.0, 6.0, ((1, 8),))
    lengths = draw_lengths(jax.random.fold_in(splits[16], 71), 0)
    order = jax.random.permutation(splits[4], SEQS).astype(jnp.int32)
    w_query = centred(splits[5], (D, QH * HD), D ** -0.5, 0.125, ((0, 8), (1, 4)))
    w_keyval = centred(splits[6], (2, D, KVH * HD), D ** -0.5, 0.125, ((1, 8),))
    w_out = centred(splits[7], (QH * HD, D), (QH * HD) ** -0.5, 0.125, ((0, 4), (1, 8)))
    w_left = centred(splits[8], (D, LRANK), D ** -0.5, 0.125, ((0, 8),))
    w_right = centred(splits[9], (LRANK, D), LRANK ** -0.5, 0.75, ((1, 8),))
    w_gateup = centred(splits[10], (2, D, FF), D ** -0.5, 0.125, ((1, 8), (2, 4)))
    w_down = centred(splits[11], (FF, D), FF ** -0.5, 0.0625, ((0, 4), (1, 8)))
    w_pergate = centred(splits[12], (D, PLDIM), D ** -0.5, 0.125, ((0, 8),))
    w_perproj = centred(splits[13], (PLDIM, D), PLDIM ** -0.5, 0.375, ((1, 8),))
    gains = jnp.clip(1.0 + 0.1 * jax.random.normal(splits[14], (6, D), jnp.float32), 0.5, 1.5)
    head_gains = jnp.clip(jax.random.uniform(splits[15], (2, HD), jnp.float32, 0.25, 0.45), 0.25, 0.45)
    return {"hidden_in": hidden_in, "layer_inputs": layer_inputs, "out_grad": out_grad, "lengths": lengths, "order": order, "w_query": w_query, "w_keyval": w_keyval, "w_out": w_out, "w_left": w_left, "w_right": w_right, "w_gateup": w_gateup, "w_down": w_down, "w_pergate": w_pergate, "w_perproj": w_perproj, "gains": gains, "head_gains": head_gains}


@jax.custom_vjp
def low(v):
    return lax.optimization_barrier(v.astype(jnp.bfloat16)).astype(jnp.float32)

@jax.custom_vjp
def low_back(v):
    return v

def low_keep(v):
    return (low(v), None)

def low_pass(kept, grad):
    return (grad,)

def back_keep(v):
    return (v, None)

def back_low(kept, grad):
    return (low(grad),)
low.defvjp(low_keep, low_pass)
low_back.defvjp(back_keep, back_low)
precise = lax.Precision.HIGHEST
half_root = 0.7071067811865476
masked_value = -1e+30

def normed(values_in, gain_vec):
    norm_scale = lax.rsqrt(lax.optimization_barrier(jnp.mean(values_in * values_in, axis=-1, keepdims=True)) + 1e-06)
    return values_in * norm_scale * gain_vec

def rotate(values_in, angles):
    half_dim = values_in.shape[-1] // 2
    first_half = values_in[..., :half_dim]
    second_half = values_in[..., half_dim:]
    cosine = jnp.cos(angles)
    sine_part = jnp.sin(angles)
    return jnp.concatenate([first_half * cosine - second_half * sine_part, second_half * cosine + first_half * sine_part], axis=-1)

def gelu_tanh(values_in):
    return jax.nn.gelu(values_in, approximate=True)

def matmul(left_mat, right_mat):
    return jnp.dot(left_mat, right_mat, precision=precise, preferred_element_type=jnp.float32)

def frequencies():
    half_dim = HD // 2
    return jnp.power(10000.0, -2.0 * jnp.arange(half_dim, dtype=jnp.float32) / HD)

def token_places(lengths, order):
    given_len = jnp.take(lengths, order)
    given_start = (jnp.cumsum(given_len) - given_len).astype(jnp.int32)
    stream = jnp.arange(TOKENS, dtype=jnp.int32)
    seq_of = lax.optimization_barrier(jnp.sum((stream[:, None] >= given_start[None, 1:]).astype(jnp.int32), axis=1)).astype(jnp.int32)
    return (seq_of, (stream - jnp.take(given_start, seq_of)).astype(jnp.int32))

def attention(queries, keys, values, seg_of, pos_of):
    blocks = TOKENS // WIN
    group_size = QH // N_TENSOR
    pad_rows = jnp.zeros((WIN,) + keys.shape[1:], jnp.float32)
    key_pad = jnp.concatenate([pad_rows, keys], axis=0)
    value_pad = jnp.concatenate([pad_rows, values], axis=0)
    seg_pad = jnp.concatenate([jnp.full((WIN,), -1, jnp.int32), seg_of], axis=0)
    pos_pad = jnp.concatenate([jnp.zeros((WIN,), jnp.int32), pos_of], axis=0)

    def one_block(block_id):
        offset = block_id * WIN
        query_block = lax.dynamic_slice_in_dim(queries, offset, WIN, 0)
        key_block = jnp.repeat(lax.dynamic_slice_in_dim(key_pad, offset, 2 * WIN, 0), group_size, axis=1)
        value_block = jnp.repeat(lax.dynamic_slice_in_dim(value_pad, offset, 2 * WIN, 0), group_size, axis=1)
        seg_query = lax.dynamic_slice_in_dim(seg_of, offset, WIN, 0)
        pos_query = lax.dynamic_slice_in_dim(pos_of, offset, WIN, 0)
        seg_key = lax.dynamic_slice_in_dim(seg_pad, offset, 2 * WIN, 0)
        pos_key = lax.dynamic_slice_in_dim(pos_pad, offset, 2 * WIN, 0)
        scores = low_back(jnp.einsum('qhd,khd->hqk', query_block, key_block, precision=precise))
        gap = pos_query[:, None] - pos_key[None, :]
        allowed = (seg_query[:, None] == seg_key[None, :]) & (gap >= 0) & (gap < WIN)
        masked = jnp.where(allowed[None], scores, masked_value)
        top_score = lax.optimization_barrier(jnp.max(masked, axis=-1, keepdims=True))
        exp_scores = jnp.exp(masked - top_score)
        probs = low(exp_scores / lax.optimization_barrier(jnp.sum(exp_scores, axis=-1, keepdims=True)))
        return jnp.einsum('hqk,khd->qhd', probs, value_block, precision=precise)
    result = lax.map(jax.checkpoint(one_block), jnp.arange(blocks, dtype=jnp.int32))
    return result.reshape(TOKENS, QH * HD)

def layer(inputs, layer_in, w_query, w_keyval, w_out, w_left, w_right, w_gateup, w_down, w_pergate, w_perproj, gains, head_gains, seg_of, pos_of):
    normal_in = normed(inputs, gains[0])
    low_in = low(normal_in)
    query_raw = low_back(matmul(low_in, w_query)).reshape(TOKENS, QH, HD)
    key_raw = matmul(low_in, w_keyval[0])
    value_raw = matmul(low_in, w_keyval[1])
    angles = pos_of.astype(jnp.float32)[:, None] * frequencies()
    queries = low(rotate(normed(query_raw, head_gains[0]), angles[:, None, :]))
    per_head = N_TENSOR // KVH
    key_list = []
    value_list = []
    for group_id in range(N_TENSOR):
        head_cols = group_id // per_head * HD
        key_copy = low_back(key_raw[:, head_cols:head_cols + HD])
        value_copy = low_back(value_raw[:, head_cols:head_cols + HD])
        key_list.append(low(rotate(normed(key_copy, head_gains[1]), angles)))
        value_list.append(low(normed(value_copy, 1.0)))
    attended = attention(queries, jnp.stack(key_list, axis=1), jnp.stack(value_list, axis=1), seg_of, pos_of)
    low_att = low(low_back(attended))
    branch = low_back(matmul(low_att, w_out))
    low_rank = low(low_back(matmul(low_in, w_left)))
    laurel_raw = low_back(matmul(low_rank, w_right))
    first_sum = (inputs + normed(branch, gains[1]) + normal_in + normed(laurel_raw, gains[2])) * half_root
    low_mid = low(normed(first_sum, gains[3]))
    gate_raw = low_back(matmul(low_mid, w_gateup[0]))
    upward = low_back(matmul(low_mid, w_gateup[1]))
    low_hidden = low(gelu_tanh(gate_raw) * upward)
    feed_raw = low_back(matmul(low_hidden, w_down))
    second_sum = first_sum + normed(feed_raw, gains[4])
    pre_gate = low_back(matmul(low(second_sum), w_pergate))
    low_gated = low(gelu_tanh(pre_gate) * layer_in)
    per_raw = low_back(matmul(low_gated, w_perproj))
    return second_sum + normed(per_raw, gains[5])

def reference(hidden_in, layer_inputs, out_grad, lengths, order, w_query, w_keyval, w_out, w_left, w_right, w_gateup, w_down, w_pergate, w_perproj, gains, head_gains):
    seg_of, pos_of = token_places(lengths, order)
    inputs = hidden_in.reshape(TOKENS, D).astype(jnp.float32)
    layer_in = layer_inputs.reshape(TOKENS, PLDIM).astype(jnp.float32)
    cotangent = out_grad.reshape(TOKENS, D).astype(jnp.float32)
    weight_list = tuple((weight_arr.astype(jnp.float32) for weight_arr in (w_query, w_keyval, w_out, w_left, w_right, w_gateup, w_down, w_pergate, w_perproj, gains, head_gains)))

    def wrapped(inputs_f, layer_f, *weight_args):
        return layer(inputs_f, layer_f, *weight_args, seg_of, pos_of)
    result, backward = jax.vjp(wrapped, inputs, layer_in, *weight_list)
    grads = backward(cotangent)
    return (result.reshape(MICRO, STRETCH, D).astype(jnp.bfloat16), grads[0].reshape(MICRO, STRETCH, D).astype(jnp.bfloat16), grads[1].reshape(MICRO, STRETCH, PLDIM).astype(jnp.bfloat16), grads[2], grads[3], grads[4], grads[5], grads[6], grads[7], grads[8], grads[9], grads[10], grads[11], grads[12])
```

```python
import jax
import jax.numpy as jnp
from jax import lax
from jax.sharding import PartitionSpec as P

KVH = 2
HD = 256
WIN = 512
LMIN = 1024
LANES = 128

half_root = 0.7071067811865476
masked_value = -1e30
bf16 = jnp.bfloat16
f32 = jnp.float32


def normed(values_in, gain_vec):
    norm_scale = lax.rsqrt(jnp.mean(values_in * values_in, axis=-1, keepdims=True) + 1e-06)
    return values_in * norm_scale * gain_vec


def rotate(values_in, angles):
    half_dim = values_in.shape[-1] // 2
    first_half = values_in[..., :half_dim]
    second_half = values_in[..., half_dim:]
    cosine = jnp.cos(angles)
    sine_part = jnp.sin(angles)
    return jnp.concatenate(
        [
            first_half * cosine - second_half * sine_part,
            second_half * cosine + first_half * sine_part,
        ],
        axis=-1,
    )


def gelu_tanh(values_in):
    return jax.nn.gelu(values_in, approximate=True)


def glu_pair(gate_raw, upward):
    return gelu_tanh(gate_raw) * upward


def value_map(raw_value):
    return normed(raw_value, 1.0)


def product(left_mat, right_mat, kind=f32):
    return jnp.dot(left_mat, right_mat, preferred_element_type=f32).astype(kind)


def against(left_mat, right_mat, kind=f32):
    return lax.dot_general(
        left_mat, right_mat, (((1,), (1,)), ((), ())), preferred_element_type=f32
    ).astype(kind)


def across(left_mat, right_mat, kind=f32):
    return lax.dot_general(
        left_mat, right_mat, (((0,), (0,)), ((), ())), preferred_element_type=f32
    ).astype(kind)


def frequencies():
    half_dim = HD // 2
    return jnp.power(10000.0, -2.0 * jnp.arange(half_dim, dtype=f32) / HD)


def shifted(piece, axis, by):
    length = lax.axis_size(axis)
    return lax.ppermute(piece, axis, [(i, (i + by) % length) for i in range(length)])


def crossed(piece, axis, bit):
    length = lax.axis_size(axis)
    return lax.ppermute(piece, axis, [(i, i ^ bit) for i in range(length)])


def spread(piece, axis):
    length = lax.axis_size(axis)
    return jnp.concatenate([piece] + [shifted(piece, axis, s) for s in range(1, length)], axis=0)


def folded(parts, axis):
    length = lax.axis_size(axis)
    rows = parts.shape[0] // length
    total = parts[:rows].astype(f32)
    for s in range(1, length):
        total = total + shifted(parts[s * rows : (s + 1) * rows], axis, -s).astype(f32)
    return total


def butterfly(piece, axis):
    length = lax.axis_size(axis)
    bit = 1
    while bit < length:
        piece = piece + crossed(piece, axis, bit)
        bit *= 2
    return piece


def passed_along(shard, axis, by):
    length = lax.axis_size(axis)
    pairs = [(i, i + by) for i in range(length) if 0 <= i + by < length]
    return lax.ppermute(shard, axis, pairs)


def blocks_of(mat, order_of):
    width = mat.shape[1] // lax.axis_size("dp")
    return jnp.concatenate(
        [lax.dynamic_slice_in_dim(mat, o * width, width, 1) for o in order_of], axis=1
    )


def rank_among(keys_own):
    count = keys_own.shape[0]
    place = jnp.arange(count, dtype=jnp.int32)
    same = (keys_own[None, :] == keys_own[:, None]) & (place[None, :] < place[:, None])
    return jnp.sum(same.astype(jnp.int32), axis=1)


def plan(lengths, order, micro, block_rows):
    devices = lax.axis_size("dp")
    parts = lax.axis_size("tensor")
    me = lax.axis_index("dp")
    part = lax.axis_index("tensor")
    tok = micro * block_rows
    own = tok // parts
    stretch = devices * block_rows
    seqs = lengths.shape[0]
    given_len = jnp.take(lengths, order)
    given_start = jnp.cumsum(given_len) - given_len
    dealt_start = jnp.cumsum(lengths) - lengths
    seq_ids = jnp.arange(seqs, dtype=jnp.int32)
    shift_given = jnp.take(dealt_start, order) - given_start
    pieces = tok // LMIN + 2
    runs = tok // stretch + 1
    per_piece = block_rows * (-(-tok // stretch)) + (parts - 1) * runs
    capacity = -(-(pieces * (per_piece // parts)) // 8) * 8
    kept = -(-(tok // parts + seqs) // 8) * 8

    def pick(table, index):
        return jnp.sum(jnp.where(index[:, None] == seq_ids[None, :], table[None, :], 0), axis=1)

    local = jnp.arange(tok, dtype=jnp.int32)
    stream = local // block_rows * stretch + me * block_rows + local % block_rows
    arrival = jnp.sum((stream[:, None] >= given_start[None, 1:]).astype(jnp.int32), axis=1)
    dealt = stream + pick(shift_given, arrival)
    target = dealt // tok
    quarter = dealt % parts
    send_slot = target * capacity + rank_among(target * parts + quarter)
    send_slot = jnp.where(quarter == part, send_slot, -1)
    keep_rank = rank_among(quarter)
    keep_slot = (part - quarter) % parts * kept + keep_rank

    place = me * tok + jnp.arange(own, dtype=jnp.int32) * parts + part
    own_seq = jnp.sum((place[:, None] >= dealt_start[None, 1:]).astype(jnp.int32), axis=1)
    shift_dealt = jnp.sum(
        jnp.where(order[None, :] == seq_ids[:, None], -shift_given[None, :], 0), axis=1
    )
    anchor = place + pick(shift_dealt, own_seq)
    source = anchor % stretch // block_rows
    prior = (anchor[None, :] < anchor[:, None]) & (source[None, :] == source[:, None])
    recv_slot = source * capacity + jnp.sum(prior.astype(jnp.int32), axis=1)

    total = devices * capacity
    slots = jnp.arange(total, dtype=jnp.int32)
    sender = (slots[:, None] == send_slot[None, :]).astype(bf16)
    receiver = (recv_slot[:, None] == slots[None, :]).astype(bf16)
    mine = jnp.where(quarter == part, keep_rank, -1)
    chosen = (jnp.arange(kept, dtype=jnp.int32)[:, None] == mine[None, :]).astype(bf16)
    compact = against(chosen, sender, bf16)
    homing = (
        keep_slot[:, None] == jnp.arange(parts * kept, dtype=jnp.int32)[None, :]
    ).astype(bf16)

    held = (part - jnp.arange(parts, dtype=jnp.int32)) % parts
    rows = (jnp.arange(own, dtype=jnp.int32)[None, :] * parts + held[:, None]).reshape(tok)
    both = me * tok + jnp.concatenate([rows - tok, rows])
    ext_seq = jnp.sum((both[:, None] >= dealt_start[None, 1:]).astype(jnp.int32), axis=1)
    ext_pos = both - pick(dealt_start, ext_seq)
    ext_seg = jnp.where(both >= 0, ext_seq, -1)
    return sender, receiver, compact, homing, ext_seg, ext_pos


def body(
    hidden_in,
    layer_inputs,
    out_grad,
    lengths,
    order,
    w_query,
    w_keyval,
    w_out,
    w_left,
    w_right,
    w_gateup,
    w_down,
    w_pergate,
    w_perproj,
    gains,
    head_gains,
):
    devices = lax.axis_size("dp")
    me = lax.axis_index("dp")
    parts = lax.axis_size("tensor")
    part = lax.axis_index("tensor")
    micro, block_rows, width = hidden_in.shape
    per_width = layer_inputs.shape[2]
    tok = micro * block_rows
    assert tok == WIN
    sender, receiver, compact, homing, ext_seg, ext_pos = plan(lengths, order, micro, block_rows)

    kv_cols = part // (parts // KVH) * HD
    kv_own = lax.dynamic_slice_in_dim(w_keyval, kv_cols, HD, 2)
    gains_high = lax.reduce_precision(gains, 8, 7)
    gains_low = (gains - gains_high).astype(bf16)
    gain_cols = jnp.concatenate([gains_high.astype(bf16), gains_low], axis=0)
    gain_cols = jnp.pad(gain_cols, ((0, LANES - gain_cols.shape[0]), (0, 0))).T
    q_width = w_query.shape[1]
    rank = w_left.shape[1]
    bundle = [
        w_query,
        kv_own[0],
        kv_own[1],
        w_out.T,
        w_left,
        w_right.T,
        w_pergate,
        w_perproj.T,
        gain_cols,
    ]
    marks = [0]
    for piece in bundle:
        marks.append(marks[-1] + piece.shape[1])
    bundle_f = lax.all_gather(jnp.concatenate(bundle, axis=1), "dp", axis=0, tiled=True)
    gathered = [bundle_f[:, a:b] for a, b in zip(marks[:-1], marks[1:])]
    wq, wk, wv, wo_t, wl, wr_t, wg, wp_t, gain_f = gathered
    gu_in, _ = lax.optimization_barrier((w_gateup, bundle_f[:8, :LANES]))
    w_gu = lax.all_gather(gu_in, "dp", axis=1, tiled=True)
    dn_in, _ = lax.optimization_barrier((w_down, w_gu[0, :8, :LANES]))
    w_dn = lax.all_gather(dn_in, "dp", axis=1, tiled=True)
    gain_rows = gain_f.T
    gains_f = gain_rows[:6].astype(f32) + gain_rows[6:12].astype(f32)

    flat = jnp.concatenate(
        [
            hidden_in.reshape(tok, width),
            layer_inputs.reshape(tok, per_width),
            out_grad.reshape(tok, width),
        ],
        axis=1,
    )
    packed = product(sender, flat, bf16)
    first_cols = width + per_width
    come_in = lax.all_to_all(packed[:, :width], "dp", 0, 0, tiled=True)
    come_rest = lax.all_to_all(packed[:, width:], "dp", 0, 0, tiled=True)
    inputs = product(receiver, come_in, bf16).astype(f32)
    rest = product(receiver, come_rest, bf16)
    layer_in = rest[:, :per_width].astype(f32)
    cotangent = rest[:, per_width:].astype(f32)

    angles = ext_pos[tok:].astype(f32)[:, None] * frequencies()

    normal_in = normed(inputs, gains_f[0])
    low_in = normal_in.astype(bf16)
    all_in = spread(low_in, "tensor")
    query_raw = product(all_in, wq).reshape(tok, -1, HD)
    key_raw = product(all_in, wk)
    value_raw = product(all_in, wv)

    def query_map(raw_value, gain_vec):
        return rotate(normed(raw_value, gain_vec), angles[:, None, :])

    def key_map(raw_value, gain_vec):
        return rotate(normed(raw_value, gain_vec), angles)

    queries = query_map(query_raw, head_gains[0]).astype(bf16)
    keys = key_map(key_raw, head_gains[1]).astype(bf16)
    values = value_map(value_raw).astype(bf16)
    tails = passed_along(jnp.concatenate([keys, values], axis=1), "dp", 1)
    ext_keys = jnp.concatenate([tails[:, :HD], keys], axis=0)
    ext_vals = jnp.concatenate([tails[:, HD:], values], axis=0)
    gap = ext_pos[tok:, None] - ext_pos[None, :]
    allowed = (ext_seg[tok:, None] == ext_seg[None, :]) & (gap >= 0) & (gap < WIN)
    scores = jnp.einsum("qhd,kd->hqk", queries, ext_keys, preferred_element_type=f32)
    masked = jnp.where(allowed[None], scores, masked_value)
    top_score = jnp.max(masked, axis=-1, keepdims=True)
    exp_scores = jnp.exp(masked - top_score)
    probs = exp_scores / jnp.sum(exp_scores, axis=-1, keepdims=True)
    low_probs = probs.astype(bf16)
    attended = jnp.einsum("hqk,kd->qhd", low_probs, ext_vals, preferred_element_type=f32)
    low_att = attended.astype(bf16).reshape(tok, -1)
    branch = folded(against(low_att, wo_t, bf16), "tensor")

    low_rank = product(low_in, wl, bf16)
    laurel_raw = against(low_rank, wr_t)
    first_sum = (
        inputs + normed(branch, gains_f[1]) + normal_in + normed(laurel_raw, gains_f[2])
    ) * half_root
    low_mid = normed(first_sum, gains_f[3]).astype(bf16)

    all_mid = spread(low_mid, "tensor")
    gate_raw = product(all_mid, w_gu[0])
    upward = product(all_mid, w_gu[1])
    low_hidden = glu_pair(gate_raw, upward).astype(bf16)
    feed_raw = folded(product(low_hidden, w_dn, bf16), "tensor")

    second_sum = first_sum + normed(feed_raw, gains_f[4])
    low_second = second_sum.astype(bf16)
    pre_gate = product(low_second, wg)
    low_gated = (gelu_tanh(pre_gate) * layer_in).astype(bf16)
    per_raw = against(low_gated, wp_t)
    result = second_sum + normed(per_raw, gains_f[5])

    _, back_per = jax.vjp(normed, per_raw, gains_f[5])
    per_grad, grad_g5 = back_per(cotangent)
    low_per = per_grad.astype(bf16)
    gated_grad = product(low_per, wp_t)
    grad_perproj = across(low_per, low_gated, bf16)
    gelu_out, back_gelu = jax.vjp(gelu_tanh, pre_gate)
    low_pre = back_gelu(gated_grad * layer_in)[0].astype(bf16)
    layer_grad = gated_grad * gelu_out
    grad_pergate = across(low_second, low_pre, bf16)
    second_grad = cotangent + against(low_pre, wg)
    _, back_feed = jax.vjp(normed, feed_raw, gains_f[4])
    feed_grad, grad_g4 = back_feed(second_grad)
    low_feed = feed_grad.astype(bf16)

    all_feed = spread(low_feed, "tensor")
    hidden_grad = against(all_feed, w_dn)
    _, back_glu = jax.vjp(glu_pair, gate_raw, upward)
    gate_grad, up_grad = back_glu(hidden_grad)
    low_gate = gate_grad.astype(bf16)
    low_up = up_grad.astype(bf16)
    mid_part = against(low_gate, w_gu[0]) + against(low_up, w_gu[1])
    mid_grad = folded(mid_part.astype(bf16), "tensor")

    _, back_mid = jax.vjp(normed, first_sum, gains_f[3])
    first_part, grad_g3 = back_mid(mid_grad)
    shared = (second_grad + first_part) * half_root
    _, back_laurel = jax.vjp(normed, laurel_raw, gains_f[2])
    laurel_grad, grad_g2 = back_laurel(shared)
    low_laurel = laurel_grad.astype(bf16)
    low_rank_grad = product(low_laurel, wr_t, bf16)
    grad_right = across(low_laurel, low_rank, bf16)
    grad_left = across(low_in, low_rank_grad, bf16)
    _, back_branch = jax.vjp(normed, branch, gains_f[1])
    branch_grad, grad_g1 = back_branch(shared)
    low_branch = branch_grad.astype(bf16)

    all_branch = spread(low_branch, "tensor")
    low_att_grad = product(all_branch, wo_t, bf16).reshape(tok, -1, HD)
    value_grad = jnp.einsum("hqk,qhd->kd", low_probs, low_att_grad, preferred_element_type=f32)
    prob_grad = jnp.einsum("qhd,kd->hqk", low_att_grad, ext_vals, preferred_element_type=f32)
    centre = jnp.sum(probs * prob_grad, axis=-1, keepdims=True)
    score_grad = (probs * (prob_grad - centre)).astype(bf16)
    query_grad = jnp.einsum("hqk,kd->qhd", score_grad, ext_keys, preferred_element_type=f32)
    key_grad = jnp.einsum("hqk,qhd->kd", score_grad, queries, preferred_element_type=f32)
    both_grad = jnp.concatenate([key_grad, value_grad], axis=1)
    from_next = passed_along(both_grad[:tok].astype(bf16), "dp", -1)
    both_total = both_grad[tok:] + from_next.astype(f32)
    _, back_query = jax.vjp(query_map, query_raw, head_gains[0])
    query_raw_grad, grad_hq = back_query(query_grad)
    _, back_key = jax.vjp(key_map, key_raw, head_gains[1])
    key_raw_grad, grad_hk = back_key(both_total[:, :HD])
    _, back_value = jax.vjp(value_map, value_raw)
    value_raw_grad = back_value(both_total[:, HD:])[0]
    low_q = query_raw_grad.reshape(tok, -1).astype(bf16)
    low_k = key_raw_grad.astype(bf16)
    low_v = value_raw_grad.astype(bf16)
    attn_part = against(low_q, wq) + against(low_k, wk) + against(low_v, wv)
    in_attn = folded(attn_part.astype(bf16), "tensor")
    normal_grad = in_attn + against(low_rank_grad, wl) + shared
    _, back_in = jax.vjp(normed, inputs, gains_f[0])
    in_part, grad_g0 = back_in(normal_grad)
    input_grad = shared + in_part

    s_gateup = lax.psum_scatter(
        jnp.stack([across(all_mid, low_gate, bf16), across(all_mid, low_up, bf16)]),
        "dp",
        scatter_dimension=1,
        tiled=True,
    )
    s_down = lax.psum_scatter(
        across(low_hidden, all_feed, bf16), "dp", scatter_dimension=1, tiled=True
    )
    gain_part = jnp.stack([grad_g1, grad_g2, grad_g3, grad_g4, grad_g5]).astype(bf16)
    gain_part = jnp.pad(gain_part, ((0, LANES - 5), (0, 0))).T
    small = jnp.concatenate(
        [grad_left, grad_right, grad_pergate, grad_perproj, gain_part], axis=1
    )
    s_small = lax.psum_scatter(small, "dp", scatter_dimension=0, tiled=True)
    attn_grads = jnp.concatenate(
        [
            across(all_in, low_q, bf16),
            across(all_in, low_k, bf16),
            across(all_in, low_v, bf16),
            across(all_branch, low_att, bf16),
        ],
        axis=1,
    )
    s_attn = lax.psum_scatter(attn_grads, "dp", scatter_dimension=0, tiled=True)

    shard_gateup = s_gateup.astype(f32)
    shard_down = s_down.astype(f32)
    small_sum = butterfly(s_small.astype(f32), "tensor")
    o_left, o_right, o_gate, o_proj = (
        rank,
        2 * rank,
        2 * rank + per_width,
        2 * rank + 2 * per_width,
    )
    shard_left = small_sum[:, :o_left]
    shard_right = small_sum[:, o_left:o_right].T
    shard_pergate = small_sum[:, o_right:o_gate]
    shard_perproj = small_sum[:, o_gate:o_proj].T
    gains_rest = small_sum[:, o_proj : o_proj + 5].T
    g0_sum = butterfly(grad_g0, "tensor")
    g0_own = lax.psum_scatter(g0_sum.reshape(1, -1), "dp", scatter_dimension=1, tiled=True)
    shard_gains = jnp.concatenate([g0_own, gains_rest], axis=0)
    shard_query = s_attn[:, :q_width].astype(f32)
    kv_part = s_attn[:, q_width : q_width + 2 * HD]
    shard_out = s_attn[:, q_width + 2 * HD :].T.astype(f32)
    group = parts // KVH
    bit = 1
    kv_sum = kv_part
    while bit < group:
        kv_sum = (kv_sum.astype(f32) + crossed(kv_sum, "tensor", bit).astype(f32)).astype(bf16)
        bit *= 2
    kv_other = crossed(kv_sum, "tensor", group)
    upper = part // group == 1
    low_head = jnp.where(upper, kv_other, kv_sum).astype(f32)
    high_head = jnp.where(upper, kv_sum, kv_other).astype(f32)
    shard_keyval = jnp.stack(
        [
            jnp.concatenate([low_head[:, :HD], high_head[:, :HD]], axis=1),
            jnp.concatenate([low_head[:, HD:], high_head[:, HD:]], axis=1),
        ]
    )
    head_total = butterfly(butterfly(jnp.stack([grad_hq, grad_hk]), "tensor"), "dp")

    def home(rows_own):
        arrived = lax.all_to_all(across(receiver, rows_own, bf16), "dp", 0, 0, tiled=True)
        shared_rows = spread(product(compact, arrived, bf16), "tensor")
        return product(homing, shared_rows, bf16)

    back_one = home(jnp.concatenate([result.astype(bf16), layer_grad.astype(bf16)], axis=1))
    back_two = home(input_grad.astype(bf16))
    return (
        back_one[:, :width].reshape(micro, block_rows, width),
        back_two.reshape(micro, block_rows, width),
        back_one[:, width:].reshape(micro, block_rows, per_width),
        shard_query,
        shard_keyval,
        shard_out,
        shard_left,
        shard_right,
        shard_gateup,
        shard_down,
        shard_pergate,
        shard_perproj,
        shard_gains,
        head_total,
    )


def solution(mesh):
    placed = (
        P(None, "dp", None),
        P(None, "dp", None),
        P(None, "dp", None),
        P(),
        P(),
        P("dp", "tensor"),
        P(None, "dp", None),
        P("tensor", "dp"),
        P("dp", None),
        P(None, "dp"),
        P(None, "dp", "tensor"),
        P("tensor", "dp"),
        P("dp", None),
        P(None, "dp"),
        P(None, "dp"),
        P(),
    )
    return jax.shard_map(
        body,
        mesh=mesh,
        in_specs=placed,
        out_specs=(
            P(None, "dp", None),
            P(None, "dp", None),
            P(None, "dp", None),
            P("dp", "tensor"),
            P(None, "dp", None),
            P("tensor", "dp"),
            P("dp", None),
            P(None, "dp"),
            P(None, "dp", "tensor"),
            P("tensor", "dp"),
            P("dp", None),
            P(None, "dp"),
            P(None, "dp"),
            P(),
        ),
        check_vma=False,
    )
```

```python
import jax
import jax.numpy as jnp
from jax import lax
from jax.experimental import pallas as pl
from jax.experimental.pallas import tpu as pltpu
from jax.sharding import PartitionSpec as P

KVH = 2
HD = 256
WIN = 512
LMIN = 1024
LANES = 128

half_root = 0.7071067811865476
masked_value = -1e30
bf16 = jnp.bfloat16
f32 = jnp.float32


def normed(values_in, gain_vec):
    norm_scale = lax.rsqrt(jnp.mean(values_in * values_in, axis=-1, keepdims=True) + 1e-06)
    return values_in * norm_scale * gain_vec


def rotate(values_in, angles):
    half_dim = values_in.shape[-1] // 2
    first_half = values_in[..., :half_dim]
    second_half = values_in[..., half_dim:]
    cosine = jnp.cos(angles)
    sine_part = jnp.sin(angles)
    return jnp.concatenate(
        [
            first_half * cosine - second_half * sine_part,
            second_half * cosine + first_half * sine_part,
        ],
        axis=-1,
    )


def gelu_tanh(values_in):
    return jax.nn.gelu(values_in, approximate=True)


def glu_pair(gate_raw, upward):
    return gelu_tanh(gate_raw) * upward


def value_map(raw_value):
    return normed(raw_value, 1.0)


def product(left_mat, right_mat, kind=f32):
    return jnp.dot(left_mat, right_mat, preferred_element_type=f32).astype(kind)


def against(left_mat, right_mat, kind=f32):
    return lax.dot_general(
        left_mat, right_mat, (((1,), (1,)), ((), ())), preferred_element_type=f32
    ).astype(kind)


def across(left_mat, right_mat, kind=f32):
    return lax.dot_general(
        left_mat, right_mat, (((0,), (0,)), ((), ())), preferred_element_type=f32
    ).astype(kind)


def frequencies():
    half_dim = HD // 2
    return jnp.power(10000.0, -2.0 * jnp.arange(half_dim, dtype=f32) / HD)


MIB = 1 << 20


def small_cost(flops):
    return pl.CostEstimate(flops=flops, bytes_accessed=1024, transcendentals=0)


def whole(shape):
    zeros = (0,) * len(shape)
    return pl.BlockSpec(shape, lambda *_: zeros, pipeline_mode=pl.Buffered(1))


def attend(queries, keys, values, low_bound, high_bound, key_place):
    tok, total = queries.shape
    heads = total // HD
    span = keys.shape[0]
    rows = 256

    def kernel(q_ref, k_ref, v_ref, lo_ref, hi_ref, kp_ref, o_ref):
        scores = against(q_ref[...], k_ref[...])
        kp = kp_ref[...]
        allowed = (kp >= lo_ref[...]) & (kp <= hi_ref[...])
        masked = jnp.where(allowed, scores, masked_value)
        raised = jnp.exp(masked - jnp.max(masked, axis=1, keepdims=True))
        inverse = 1.0 / jnp.sum(raised, axis=1, keepdims=True)
        o_ref[...] = product((raised * inverse).astype(bf16), v_ref[...], bf16)

    return pl.pallas_call(
        kernel,
        out_shape=jax.ShapeDtypeStruct((tok, total), bf16),
        grid=(heads, tok // rows),
        in_specs=[
            pl.BlockSpec((rows, HD), lambda h, i: (i, h)),
            whole((span, HD)),
            whole((span, HD)),
            pl.BlockSpec((rows, 1), lambda h, i: (i, 0)),
            pl.BlockSpec((rows, 1), lambda h, i: (i, 0)),
            whole((1, span)),
        ],
        out_specs=pl.BlockSpec((rows, HD), lambda h, i: (i, h)),
        compiler_params=pltpu.CompilerParams(vmem_limit_bytes=32 * MIB),
        cost_estimate=small_cost(4 * tok * span * total),
        name="attend",
    )(queries, keys, values, low_bound[:, None], high_bound[:, None], key_place[None, :])


def attend_back(queries, keys, values, out_grad, low_bound, high_bound, key_place):
    tok, total = queries.shape
    heads = total // HD
    span = keys.shape[0]
    rows = 256

    def kernel(q_ref, k_ref, v_ref, g_ref, lo_ref, hi_ref, kp_ref, dq_ref, dk_ref, dv_ref):
        first = (pl.program_id(0) == 0) & (pl.program_id(1) == 0)
        q, k, v, g = q_ref[...], k_ref[...], v_ref[...], g_ref[...]
        scores = against(k, q)
        kp = kp_ref[...]
        allowed = (kp >= lo_ref[...]) & (kp <= hi_ref[...])
        masked = jnp.where(allowed, scores, masked_value)
        raised = jnp.exp(masked - jnp.max(masked, axis=0, keepdims=True))
        probs = raised * (1.0 / jnp.sum(raised, axis=0, keepdims=True))
        prob_grad = against(v, g)
        centre = jnp.sum(probs * prob_grad, axis=0, keepdims=True)
        score_grad = (probs * (prob_grad - centre)).astype(bf16)
        dq_ref[...] = across(score_grad, k)
        dk_part = product(score_grad, q)
        dv_part = product(probs.astype(bf16), g)

        @pl.when(first)
        def _():
            dk_ref[...] = dk_part
            dv_ref[...] = dv_part

        @pl.when(jnp.logical_not(first))
        def _():
            dk_ref[...] += dk_part
            dv_ref[...] += dv_part

    return pl.pallas_call(
        kernel,
        out_shape=(
            jax.ShapeDtypeStruct((tok, total), f32),
            jax.ShapeDtypeStruct((span, HD), f32),
            jax.ShapeDtypeStruct((span, HD), f32),
        ),
        grid=(heads, tok // rows),
        in_specs=[
            pl.BlockSpec((rows, HD), lambda h, i: (i, h)),
            whole((span, HD)),
            whole((span, HD)),
            pl.BlockSpec((rows, HD), lambda h, i: (i, h)),
            pl.BlockSpec((1, rows), lambda h, i: (0, i)),
            pl.BlockSpec((1, rows), lambda h, i: (0, i)),
            whole((span, 1)),
        ],
        out_specs=(
            pl.BlockSpec((rows, HD), lambda h, i: (i, h)),
            pl.BlockSpec((span, HD), lambda h, i: (0, 0)),
            pl.BlockSpec((span, HD), lambda h, i: (0, 0)),
        ),
        compiler_params=pltpu.CompilerParams(vmem_limit_bytes=40 * MIB),
        cost_estimate=small_cost(10 * tok * span * total),
        name="attend_back",
    )(
        queries,
        keys,
        values,
        out_grad,
        low_bound[None, :],
        high_bound[None, :],
        key_place[:, None],
    )


def feed_forward(mid, w_ff, units):
    tok, width = mid.shape
    blk = 512

    def kernel(m_ref, g_ref, u_ref, d_ref, gate_ref, up_ref, hid_ref, out_ref, acc):
        step = pl.program_id(0)
        mid_rows = m_ref[...]
        gate = product(mid_rows, g_ref[...])
        up = product(mid_rows, u_ref[...])
        hidden = glu_pair(gate, up).astype(bf16)
        gate_ref[...] = gate.astype(bf16)
        up_ref[...] = up.astype(bf16)
        hid_ref[...] = hidden
        part = against(hidden, d_ref[...])

        @pl.when(step == 0)
        def _():
            acc[...] = part

        @pl.when(step > 0)
        def _():
            acc[...] += part

        @pl.when(step == pl.num_programs(0) - 1)
        def _():
            out_ref[...] = acc[...].astype(bf16)

    plane = lambda k: pl.BlockSpec((width, blk), lambda j: (0, k * (units // blk) + j))
    columns = pl.BlockSpec((tok, blk), lambda j: (0, j))
    return pl.pallas_call(
        kernel,
        out_shape=[jax.ShapeDtypeStruct((tok, units), bf16)] * 3
        + [jax.ShapeDtypeStruct((tok, width), bf16)],
        grid=(units // blk,),
        in_specs=[whole((tok, width)), plane(0), plane(1), plane(2)],
        out_specs=[columns, columns, columns, pl.BlockSpec((tok, width), lambda j: (0, 0))],
        scratch_shapes=[pltpu.VMEM((tok, width), f32)],
        compiler_params=pltpu.CompilerParams(vmem_limit_bytes=56 * MIB),
        cost_estimate=small_cost(6 * tok * width * units),
        name="feed_forward",
    )(mid, w_ff, w_ff, w_ff)


def feed_back(feed, w_ff, gate_raw, upward):
    tok, width = feed.shape
    units = upward.shape[1]
    blk = 512

    def kernel(f_ref, g_ref, u_ref, d_ref, gate_ref, up_ref, all_ref, out_ref, acc):
        step = pl.program_id(0)
        hidden_grad = product(f_ref[...], d_ref[...])
        gate = gate_ref[...].astype(f32)
        _, back_glu = jax.vjp(glu_pair, gate, up_ref[...].astype(f32))
        gate_grad, up_grad = back_glu(hidden_grad)
        low_gate, low_up = gate_grad.astype(bf16), up_grad.astype(bf16)
        all_ref[0] = low_gate
        all_ref[1] = low_up
        part = against(low_gate, g_ref[...]) + against(low_up, u_ref[...])

        @pl.when(step == 0)
        def _():
            acc[...] = part

        @pl.when(step > 0)
        def _():
            acc[...] += part

        @pl.when(step == pl.num_programs(0) - 1)
        def _():
            out_ref[...] = acc[...].astype(bf16)

    plane = lambda k: pl.BlockSpec((width, blk), lambda j: (0, k * (units // blk) + j))
    columns = pl.BlockSpec((tok, blk), lambda j: (0, j))
    return pl.pallas_call(
        kernel,
        out_shape=(
            jax.ShapeDtypeStruct((2, tok, units), bf16),
            jax.ShapeDtypeStruct((tok, width), bf16),
        ),
        grid=(units // blk,),
        in_specs=[whole((tok, width)), plane(0), plane(1), plane(2), columns, columns],
        out_specs=(
            pl.BlockSpec((2, tok, blk), lambda j: (0, 0, j)),
            pl.BlockSpec((tok, width), lambda j: (0, 0)),
        ),
        scratch_shapes=[pltpu.VMEM((tok, width), f32)],
        compiler_params=pltpu.CompilerParams(vmem_limit_bytes=56 * MIB),
        cost_estimate=small_cost(6 * tok * width * units),
        name="feed_back",
    )(feed, w_ff, w_ff, w_ff, gate_raw, upward)


def feed_grads(left_mat, planes):
    tok, width = left_mat.shape
    count, _, units = planes.shape
    blk = 256

    def kernel(l_ref, p_ref, o_ref):
        o_ref[...] = across(l_ref[...], p_ref[...], bf16)

    return pl.pallas_call(
        kernel,
        out_shape=jax.ShapeDtypeStruct((count, width, units), bf16),
        grid=(count, width // blk),
        in_specs=[
            pl.BlockSpec((tok, blk), lambda w, i: (0, i)),
            pl.BlockSpec((None, tok, units), lambda w, i: (w, 0, 0)),
        ],
        out_specs=pl.BlockSpec((None, blk, units), lambda w, i: (w, i, 0)),
        compiler_params=pltpu.CompilerParams(vmem_limit_bytes=32 * MIB),
        cost_estimate=small_cost(1024),
        name="feed_grads",
    )(left_mat, planes)


def attention_grads(all_in, all_branch, low_qkv, low_att):
    tok, width = all_in.shape
    first, second = low_qkv.shape[1], low_att.shape[1]
    blk = 256

    def kernel(i_ref, b_ref, q_ref, a_ref, o_ref):
        o_ref[:, :first] = across(i_ref[...], q_ref[...], bf16)
        o_ref[:, first:] = across(b_ref[...], a_ref[...], bf16)

    return pl.pallas_call(
        kernel,
        out_shape=jax.ShapeDtypeStruct((width, first + second), bf16),
        grid=(width // blk,),
        in_specs=[
            pl.BlockSpec((tok, blk), lambda i: (0, i)),
            pl.BlockSpec((tok, blk), lambda i: (0, i)),
            whole((tok, first)),
            whole((tok, second)),
        ],
        out_specs=pl.BlockSpec((blk, first + second), lambda i: (i, 0)),
        compiler_params=pltpu.CompilerParams(vmem_limit_bytes=32 * MIB),
        cost_estimate=small_cost(1024),
        name="attention_grads",
    )(all_in, all_branch, low_qkv, low_att)


def shifted(piece, axis, by):
    length = lax.axis_size(axis)
    return lax.ppermute(piece, axis, [(i, (i + by) % length) for i in range(length)])


def crossed(piece, axis, bit):
    length = lax.axis_size(axis)
    return lax.ppermute(piece, axis, [(i, i ^ bit) for i in range(length)])


def spread(piece, axis):
    length = lax.axis_size(axis)
    return jnp.concatenate([piece] + [shifted(piece, axis, s) for s in range(1, length)], axis=0)


def spread_start(piece, axis):
    length = lax.axis_size(axis)
    return [shifted(piece, axis, s) for s in range(1, length)]


def fold_start(parts, axis):
    length = lax.axis_size(axis)
    rows = parts.shape[0] // length
    return [parts[:rows]] + [
        shifted(parts[s * rows : (s + 1) * rows], axis, -s) for s in range(1, length)
    ]


def folded(parts, axis):
    return summed(fold_start(parts, axis))


def with_work(arrived, work):
    return lax.optimization_barrier((arrived, work))


def butterfly(piece, axis):
    length = lax.axis_size(axis)
    bit = 1
    while bit < length:
        piece = piece.astype(bf16)
        piece = piece.astype(f32) + crossed(piece, axis, bit).astype(f32)
        bit *= 2
    return piece


def passed_along(shard, axis, by):
    length = lax.axis_size(axis)
    pairs = [(i, i + by) for i in range(length) if 0 <= i + by < length]
    return lax.ppermute(shard, axis, pairs)


def summed(terms):
    total = terms[0].astype(f32)
    for term in terms[1:]:
        total = total + term.astype(f32)
    return total


def rank_among(keys_own):
    count = keys_own.shape[0]
    place = jnp.arange(count, dtype=jnp.int32)
    same = (keys_own[None, :] == keys_own[:, None]) & (place[None, :] < place[:, None])
    return jnp.sum(same.astype(jnp.int32), axis=1)


def plan(lengths, order, micro, block_rows):
    devices = lax.axis_size("dp")
    parts = lax.axis_size("tensor")
    me = lax.axis_index("dp")
    part = lax.axis_index("tensor")
    tok = micro * block_rows
    own = tok // parts
    stretch = devices * block_rows
    seqs = lengths.shape[0]
    given_len = jnp.take(lengths, order)
    given_start = jnp.cumsum(given_len) - given_len
    dealt_start = jnp.cumsum(lengths) - lengths
    seq_ids = jnp.arange(seqs, dtype=jnp.int32)
    shift_given = jnp.take(dealt_start, order) - given_start
    pieces = tok // LMIN + 2
    runs = tok // stretch + 1
    per_piece = block_rows * (-(-tok // stretch)) + (parts - 1) * runs
    capacity = -(-(pieces * (per_piece // parts) + 1) // 8) * 8
    kept = -(-(tok // parts + seqs + 1) // 8) * 8

    def pick(table, index):
        return jnp.sum(jnp.where(index[:, None] == seq_ids[None, :], table[None, :], 0), axis=1)

    local = jnp.arange(tok, dtype=jnp.int32)
    stream = local // block_rows * stretch + me * block_rows + local % block_rows
    arrival = jnp.sum((stream[:, None] >= given_start[None, 1:]).astype(jnp.int32), axis=1)
    dealt = stream + pick(shift_given, arrival)
    target = dealt // tok
    quarter = dealt % parts
    send_slot = target * capacity + rank_among(target * parts + quarter)
    send_slot = jnp.where(quarter == part, send_slot, -1)
    keep_rank = rank_among(quarter)
    keep_slot = (part - quarter) % parts * kept + keep_rank

    place = me * tok + jnp.arange(own, dtype=jnp.int32) * parts + part
    own_seq = jnp.sum((place[:, None] >= dealt_start[None, 1:]).astype(jnp.int32), axis=1)
    shift_dealt = jnp.sum(
        jnp.where(order[None, :] == seq_ids[:, None], -shift_given[None, :], 0), axis=1
    )
    anchor = place + pick(shift_dealt, own_seq)
    source = anchor % stretch // block_rows
    prior = (anchor[None, :] < anchor[:, None]) & (source[None, :] == source[:, None])
    recv_slot = source * capacity + jnp.sum(prior.astype(jnp.int32), axis=1)

    total = devices * capacity
    slots = jnp.arange(total, dtype=jnp.int32)
    sender = (slots[:, None] == send_slot[None, :]).astype(bf16)
    receiver = (recv_slot[:, None] == slots[None, :]).astype(bf16)
    mine = jnp.where(quarter == part, keep_rank, -1)
    chosen = (jnp.arange(kept, dtype=jnp.int32)[:, None] == mine[None, :]).astype(bf16)
    compact = against(chosen, sender, bf16)
    homing = (
        keep_slot[:, None] == jnp.arange(parts * kept, dtype=jnp.int32)[None, :]
    ).astype(bf16)

    held = (part - jnp.arange(parts, dtype=jnp.int32)) % parts
    rows = (jnp.arange(own, dtype=jnp.int32)[None, :] * parts + held[:, None]).reshape(tok)
    both = me * tok + jnp.concatenate([rows - tok, rows])
    ext_seq = jnp.sum((both[:, None] >= dealt_start[None, 1:]).astype(jnp.int32), axis=1)
    start = pick(dealt_start, ext_seq[tok:])
    high_bound = both[tok:]
    low_bound = jnp.maximum(start, high_bound - (WIN - 1))
    return sender, receiver, compact, homing, (low_bound, high_bound, both), high_bound - start


def body(
    hidden_in,
    layer_inputs,
    out_grad,
    lengths,
    order,
    w_query,
    w_keyval,
    w_out,
    w_left,
    w_right,
    w_gateup,
    w_down,
    w_pergate,
    w_perproj,
    gains,
    head_gains,
):
    devices = lax.axis_size("dp")
    me = lax.axis_index("dp")
    parts = lax.axis_size("tensor")
    part = lax.axis_index("tensor")
    micro, block_rows, width = hidden_in.shape
    per_width = layer_inputs.shape[2]
    tok = micro * block_rows
    assert tok == WIN
    sender, receiver, compact, homing, bounds, own_pos = plan(lengths, order, micro, block_rows)

    kv_cols = part // (parts // KVH) * HD
    kv_own = lax.dynamic_slice_in_dim(w_keyval, kv_cols, HD, 2)
    gains_high = lax.reduce_precision(gains, 8, 7)
    gains_low = (gains - gains_high).astype(bf16)
    gain_cols = jnp.concatenate([gains_high.astype(bf16), gains_low], axis=0)
    gain_cols = jnp.pad(gain_cols, ((0, LANES - gain_cols.shape[0]), (0, 0))).T
    q_width = w_query.shape[1]
    rank = w_left.shape[1]

    def gather_columns(pieces):
        marks = [0]
        for piece in pieces:
            marks.append(marks[-1] + piece.shape[1])
        full = lax.all_gather(jnp.concatenate(pieces, axis=1), "dp", axis=0, tiled=True)
        return full, [full[:, a:b] for a, b in zip(marks[:-1], marks[1:])]

    first = [w_query, kv_own[0], kv_own[1], w_out.T, w_left, w_right.T, gain_cols]
    bundle_a, (wq, wk, wv, wo_t, wl, wr_t, gain_f) = gather_columns(first)
    units = w_down.shape[0]
    flat = jnp.concatenate(
        [
            hidden_in.reshape(tok, width),
            layer_inputs.reshape(tok, per_width),
            out_grad.reshape(tok, width),
        ],
        axis=1,
    )
    packed = product(sender, flat, bf16)
    first_cols = width + per_width
    come_in = lax.all_to_all(packed[:, :width], "dp", 0, 0, tiled=True)
    low_inputs = product(receiver, come_in, bf16)
    inputs = low_inputs.astype(f32)
    token_pieces = spread_start(low_inputs, "tensor")
    second = [w_gateup[0], w_gateup[1], w_down.T, w_pergate, w_perproj.T]
    second[3], gain_f = with_work(second[3], gain_f)
    second[4], token_pieces[0] = with_work(second[4], token_pieces[0])
    w_ff, (_, _, _, wg, wp_t) = gather_columns(second)
    w_gains = gain_f.T
    gains_f = w_gains[:6].astype(f32) + w_gains[6:12].astype(f32)
    all_inputs = jnp.concatenate([low_inputs] + token_pieces, axis=0)

    angles = own_pos.astype(f32)[:, None] * frequencies()

    def homeward(rows_own):
        return lax.all_to_all(across(receiver, rows_own, bf16), "dp", 0, 0, tiled=True)

    all_in = normed(all_inputs.astype(f32), gains_f[0]).astype(bf16)
    normal_in = normed(inputs, gains_f[0])
    low_in = normal_in.astype(bf16)
    query_raw = product(all_in, wq).reshape(tok, -1, HD)
    key_raw = product(all_in, wk)
    value_raw = product(all_in, wv)

    def query_map(raw_value, gain_vec):
        return rotate(normed(raw_value, gain_vec), angles[:, None, :])

    def key_map(raw_value, gain_vec):
        return rotate(normed(raw_value, gain_vec), angles)

    queries = query_map(query_raw, head_gains[0]).astype(bf16)
    keys = key_map(key_raw, head_gains[1]).astype(bf16)
    values = value_map(value_raw).astype(bf16)
    tails = passed_along(jnp.concatenate([keys, values], axis=1), "dp", 1)
    ext_keys = jnp.concatenate([tails[:, :HD], keys], axis=0)
    ext_vals = jnp.concatenate([tails[:, HD:], values], axis=0)
    flat_queries = queries.reshape(tok, -1)
    low_att = attend(flat_queries, ext_keys, ext_vals, *bounds)
    branch = folded(against(low_att, wo_t, bf16), "tensor")

    low_rank = product(low_in, wl, bf16)
    laurel_raw = against(low_rank, wr_t)
    first_sum = (
        inputs + normed(branch, gains_f[1]) + normal_in + normed(laurel_raw, gains_f[2])
    ) * half_root
    low_mid = normed(first_sum, gains_f[3]).astype(bf16)

    mid_pieces = spread_start(low_mid, "tensor")
    rest_out, mid_pieces[0] = with_work(packed[:, width:], mid_pieces[0])
    rest = product(receiver, lax.all_to_all(rest_out, "dp", 0, 0, tiled=True), bf16)
    all_mid = jnp.concatenate([low_mid] + mid_pieces, axis=0)
    layer_in = rest[:, :per_width].astype(f32)
    cotangent = rest[:, per_width:].astype(f32)
    gate_raw, upward, low_hidden, feed_part = feed_forward(all_mid, w_ff, units)
    feed_raw = folded(feed_part, "tensor")

    second_sum = first_sum + normed(feed_raw, gains_f[4])
    low_second = second_sum.astype(bf16)
    pre_gate = product(low_second, wg)
    low_gated = (gelu_tanh(pre_gate) * layer_in).astype(bf16)
    per_raw = against(low_gated, wp_t)
    result = second_sum + normed(per_raw, gains_f[5])

    _, back_per = jax.vjp(normed, per_raw, gains_f[5])
    per_grad, grad_g5 = back_per(cotangent)
    low_per = per_grad.astype(bf16)
    gated_grad = product(low_per, wp_t)
    gelu_out, back_gelu = jax.vjp(gelu_tanh, pre_gate)
    low_pre = back_gelu(gated_grad * layer_in)[0].astype(bf16)
    layer_grad = gated_grad * gelu_out
    second_grad = cotangent + against(low_pre, wg)
    _, back_feed = jax.vjp(normed, feed_raw, gains_f[4])
    feed_grad, grad_g4 = back_feed(second_grad)
    low_feed = feed_grad.astype(bf16)

    feed_pieces = spread_start(low_feed, "tensor")
    grad_perproj = across(low_per, low_gated, bf16)
    grad_pergate = across(low_second, low_pre, bf16)
    low_result = jnp.concatenate([result.astype(bf16), layer_grad.astype(bf16)], axis=1)
    low_result, feed_pieces[0] = with_work(low_result, feed_pieces[0])
    come_one = homeward(low_result)
    feed_pieces, (grad_perproj, grad_pergate, come_one) = with_work(
        feed_pieces, (grad_perproj, grad_pergate, come_one)
    )
    all_feed = jnp.concatenate([low_feed] + feed_pieces, axis=0)

    home_one = product(compact, come_one, bf16)
    home_pieces = spread_start(home_one, "tensor")
    down_grads = feed_grads(all_feed, low_hidden[None])[0]
    down_grads, all_feed = with_work(down_grads, all_feed)
    s_down = lax.psum_scatter(down_grads, "dp", scatter_dimension=0, tiled=True)
    planes, mid_part = feed_back(all_feed, w_ff, gate_raw, upward)

    mid_part, home_pieces[0] = with_work(mid_part, home_pieces[0])
    mid_part, home_pieces[-1] = with_work(mid_part, home_pieces[-1])

    mid_pieces = fold_start(mid_part, "tensor")
    gu_grads = feed_grads(all_mid, planes)
    gu_grads, s_down = with_work(gu_grads, s_down)
    mid_pieces, gu_grads = with_work(mid_pieces, gu_grads)
    s_gateup = lax.psum_scatter(gu_grads, "dp", scatter_dimension=1, tiled=True)
    mid_grad = summed(mid_pieces)

    _, back_mid = jax.vjp(normed, first_sum, gains_f[3])
    first_part, grad_g3 = back_mid(mid_grad)
    shared = (second_grad + first_part) * half_root
    _, back_laurel = jax.vjp(normed, laurel_raw, gains_f[2])
    laurel_grad, grad_g2 = back_laurel(shared)
    low_laurel = laurel_grad.astype(bf16)
    _, back_branch = jax.vjp(normed, branch, gains_f[1])
    branch_grad, grad_g1 = back_branch(shared)
    low_branch = branch_grad.astype(bf16)

    branch_pieces = spread_start(low_branch, "tensor")
    low_rank_grad = product(low_laurel, wr_t, bf16)
    grad_right = across(low_laurel, low_rank, bf16)
    grad_left = across(low_in, low_rank_grad, bf16)
    small = jnp.concatenate([grad_left, grad_right, grad_pergate, grad_perproj], axis=1)
    gain_part = jnp.stack([grad_g1, grad_g2, grad_g3, grad_g4, grad_g5])
    branch_pieces, (small, gain_part) = with_work(branch_pieces, (small, gain_part))
    all_branch = jnp.concatenate([low_branch] + branch_pieces, axis=0)

    low_att_grad = product(all_branch, wo_t, bf16)
    query_grad, key_grad, value_grad = attend_back(
        flat_queries, ext_keys, ext_vals, low_att_grad, *bounds
    )
    query_grad, home_pieces[1] = with_work(query_grad, home_pieces[1])
    query_grad = query_grad.reshape(tok, -1, HD)
    both_grad = jnp.concatenate([key_grad, value_grad], axis=1)
    from_next = passed_along(both_grad[:tok].astype(bf16), "dp", -1)
    both_total = both_grad[tok:] + from_next.astype(f32)
    _, back_query = jax.vjp(query_map, query_raw, head_gains[0])
    query_raw_grad, grad_hq = back_query(query_grad)
    _, back_key = jax.vjp(key_map, key_raw, head_gains[1])
    key_raw_grad, grad_hk = back_key(both_total[:, :HD])
    _, back_value = jax.vjp(value_map, value_raw)
    value_raw_grad = back_value(both_total[:, HD:])[0]
    low_q = query_raw_grad.reshape(tok, -1).astype(bf16)
    low_k = key_raw_grad.astype(bf16)
    low_v = value_raw_grad.astype(bf16)
    attn_part = against(low_q, wq) + against(low_k, wk) + against(low_v, wv)

    in_pieces = fold_start(attn_part.astype(bf16), "tensor")
    low_qkv = jnp.concatenate([low_q, low_k, low_v], axis=1)
    at_grads = attention_grads(all_in, all_branch, low_qkv, low_att)
    head_cols = jnp.stack([grad_hq, grad_hk]).reshape(-1, width // devices)
    head_count = head_cols.shape[0]
    head_cols = jnp.tile(head_cols, (1, devices))
    last_cols = jnp.concatenate([gain_part, head_cols], axis=0).astype(bf16)
    last_cols = jnp.pad(last_cols, ((0, LANES - last_cols.shape[0]), (0, 0))).T
    at_grads = jnp.concatenate([at_grads, small, last_cols], axis=1)
    in_pieces, at_grads = with_work(in_pieces, at_grads)
    in_attn = summed(in_pieces)
    normal_grad = in_attn + against(low_rank_grad, wl) + shared
    _, back_in = jax.vjp(normed, inputs, gains_f[0])
    in_part, grad_g0 = back_in(normal_grad)
    input_grad = shared + in_part
    block = width // devices
    extra = jnp.pad(
        grad_g0.reshape(devices, 1, block),
        ((0, 0), (receiver.shape[1] // devices - 1, 0), (0, width - block)),
    )
    sent_two = across(receiver, input_grad.astype(bf16)) + extra.reshape(-1, width)
    come_two = lax.all_to_all(sent_two.astype(bf16), "dp", 0, 0, tiled=True)
    at_grads, s_gateup = with_work(at_grads, s_gateup)
    s_at = lax.psum_scatter(at_grads, "dp", scatter_dimension=0, tiled=True)
    g0_part = jnp.sum(come_two.reshape(devices, -1, width)[:, -1, :block].astype(f32), axis=0)
    home_two = product(compact, come_two) + jnp.pad(
        g0_part[None], ((compact.shape[0] - 1, 0), (0, width - block))
    )
    all_two = spread(home_two.astype(bf16), "tensor")
    back_two = product(homing, all_two, bf16)
    g0_terms = all_two.reshape(parts, -1, width)[:, -1, :block].astype(f32)
    while g0_terms.shape[0] > 1:
        middle = g0_terms.shape[0] // 2
        g0_terms = g0_terms[:middle] + g0_terms[middle:]

    shard_gateup = s_gateup.astype(f32)
    shard_down = s_down.T.astype(f32)
    o_kv = q_width + 2 * HD
    o_small = o_kv + w_out.shape[0]
    shard_query = s_at[:, :q_width].astype(f32)
    kv_part = s_at[:, q_width:o_kv]
    shard_out = s_at[:, o_kv:o_small].T.astype(f32)
    small_sum = butterfly(s_at[:, o_small:], "tensor")
    o_left, o_right, o_gate, o_proj = (
        rank,
        2 * rank,
        2 * rank + per_width,
        2 * rank + 2 * per_width,
    )
    shard_left = small_sum[:, :o_left]
    shard_right = small_sum[:, o_left:o_right].T
    shard_pergate = small_sum[:, o_right:o_gate]
    shard_perproj = small_sum[:, o_gate:o_proj].T
    last_sum = small_sum[:, o_proj:].T
    shard_gains = jnp.concatenate([g0_terms, last_sum[:5]], axis=0)
    head_total = last_sum[5 : 5 + head_count].reshape(2, HD)
    group = parts // KVH
    bit = 1
    kv_sum = kv_part
    while bit < group:
        kv_sum = (kv_sum.astype(f32) + crossed(kv_sum, "tensor", bit).astype(f32)).astype(bf16)
        bit *= 2
    kv_other = crossed(kv_sum, "tensor", group)
    upper = part // group == 1
    low_head = jnp.where(upper, kv_other, kv_sum).astype(f32)
    high_head = jnp.where(upper, kv_sum, kv_other).astype(f32)
    shard_keyval = jnp.stack(
        [
            jnp.concatenate([low_head[:, :HD], high_head[:, :HD]], axis=1),
            jnp.concatenate([low_head[:, HD:], high_head[:, HD:]], axis=1),
        ]
    )
    back_one = product(homing, jnp.concatenate([home_one] + home_pieces, axis=0), bf16)
    return (
        back_one[:, :width].reshape(micro, block_rows, width),
        back_two.reshape(micro, block_rows, width),
        back_one[:, width:].reshape(micro, block_rows, per_width),
        shard_query,
        shard_keyval,
        shard_out,
        shard_left,
        shard_right,
        shard_gateup,
        shard_down,
        shard_pergate,
        shard_perproj,
        shard_gains,
        head_total,
    )


def solution(mesh):
    placed = (
        P(None, "dp", None),
        P(None, "dp", None),
        P(None, "dp", None),
        P(),
        P(),
        P("dp", "tensor"),
        P(None, "dp", None),
        P("tensor", "dp"),
        P("dp", None),
        P(None, "dp"),
        P(None, "dp", "tensor"),
        P("tensor", "dp"),
        P("dp", None),
        P(None, "dp"),
        P(None, "dp"),
        P(),
    )
    return jax.shard_map(
        body,
        mesh=mesh,
        in_specs=placed,
        out_specs=(
            P(None, "dp", None),
            P(None, "dp", None),
            P(None, "dp", None),
            P("dp", "tensor"),
            P(None, "dp", None),
            P("tensor", "dp"),
            P("dp", None),
            P(None, "dp"),
            P(None, "dp", "tensor"),
            P("tensor", "dp"),
            P("dp", None),
            P(None, "dp"),
            P(None, "dp"),
            P(),
        ),
        check_vma=False,
    )
```

```python
import jax
import jax.numpy as jnp
from jax import lax
from jax.experimental import pallas as pl
from jax.experimental.pallas import tpu as pltpu
from jax.sharding import PartitionSpec as P

KVH = 2
HD = 256
WIN = 512
LMIN = 1024
LANES = 128

half_root = 0.7071067811865476
masked_value = -1e30
bf16 = jnp.bfloat16
f32 = jnp.float32


def normed(values_in, gain_vec):
    norm_scale = lax.rsqrt(jnp.mean(values_in * values_in, axis=-1, keepdims=True) + 1e-06)
    return values_in * norm_scale * gain_vec


def rotate(values_in, angles):
    half_dim = values_in.shape[-1] // 2
    first_half = values_in[..., :half_dim]
    second_half = values_in[..., half_dim:]
    cosine = jnp.cos(angles)
    sine_part = jnp.sin(angles)
    return jnp.concatenate(
        [
            first_half * cosine - second_half * sine_part,
            second_half * cosine + first_half * sine_part,
        ],
        axis=-1,
    )


def gelu_tanh(values_in):
    return jax.nn.gelu(values_in, approximate=True)


def glu_pair(gate_raw, upward):
    return gelu_tanh(gate_raw) * upward


def value_map(raw_value):
    return normed(raw_value, 1.0)


def product(left_mat, right_mat, kind=f32):
    return jnp.dot(left_mat, right_mat, preferred_element_type=f32).astype(kind)


def against(left_mat, right_mat, kind=f32):
    return lax.dot_general(
        left_mat, right_mat, (((1,), (1,)), ((), ())), preferred_element_type=f32
    ).astype(kind)


def across(left_mat, right_mat, kind=f32):
    return lax.dot_general(
        left_mat, right_mat, (((0,), (0,)), ((), ())), preferred_element_type=f32
    ).astype(kind)


def frequencies():
    half_dim = HD // 2
    return jnp.power(10000.0, -2.0 * jnp.arange(half_dim, dtype=f32) / HD)


MIB = 1 << 20


def small_cost(flops):
    return pl.CostEstimate(flops=flops, bytes_accessed=1024, transcendentals=0)


def whole(shape):
    zeros = (0,) * len(shape)
    return pl.BlockSpec(shape, lambda *_: zeros, pipeline_mode=pl.Buffered(1))


def in_pieces_of(count, rows, width):
    return [whole((rows, width)) for _ in range(count)]


def gather_rows(piece_refs, full_ref):
    rows = piece_refs[0].shape[0]
    for index, piece in enumerate(piece_refs):
        full_ref[index * rows : (index + 1) * rows, :] = piece[...]


def give_rows(step, value, piece_refs):
    rows = piece_refs[0].shape[0]
    each = value.shape[0] // rows
    for index, piece in enumerate(piece_refs):
        place = index % each * rows

        @pl.when(step == index // each)
        def _():
            piece[...] = value[place : place + rows, :].astype(bf16)


def mean_scale(values):
    return lax.rsqrt(jnp.mean(values * values, axis=1, keepdims=True) + 1e-06)


def turned(values, cosine, sine):
    half = values.shape[1] // 2
    first, second = values[:, :half], values[:, half:]
    return jnp.concatenate(
        [first * cosine - second * sine, second * cosine + first * sine], axis=1
    )


def project(pieces, gain, bundle, head_gains, cosine, sine, heads):
    count = len(pieces)
    own, width = pieces[0].shape
    tok = count * own
    total = (heads + 2) * HD
    rows = tok // 2

    def kernel(*refs):
        piece_refs = refs[:count]
        g_ref, w_ref, hg_ref, c_ref, s_ref, in_ref, raw_ref, q_ref, kv_ref, full = refs[count:]
        step = pl.program_id(0)

        @pl.when(step == 0)
        def _():
            gather_rows(piece_refs, full)

        x = full[pl.ds(pl.multiple_of(step * rows, rows), rows), :].astype(f32)
        low = (x * mean_scale(x) * g_ref[...]).astype(bf16)
        in_ref[...] = low
        raw = product(low, w_ref[...])
        raw_ref[...] = raw
        cosine, sine = c_ref[...], s_ref[...]
        for head in range(heads):
            part = raw[:, head * HD : (head + 1) * HD]
            part = part * mean_scale(part) * hg_ref[0:1, :]
            q_ref[:, head * HD : (head + 1) * HD] = turned(part, cosine, sine).astype(bf16)
        part = raw[:, heads * HD : (heads + 1) * HD]
        part = part * mean_scale(part) * hg_ref[1:2, :]
        kv_ref[:, :HD] = turned(part, cosine, sine).astype(bf16)
        part = raw[:, (heads + 1) * HD :]
        kv_ref[:, HD:] = (part * mean_scale(part)).astype(bf16)

    def row_block(columns):
        return pl.BlockSpec((rows, columns), lambda i: (i, 0))

    return pl.pallas_call(
        kernel,
        out_shape=(
            jax.ShapeDtypeStruct((tok, width), bf16),
            jax.ShapeDtypeStruct((tok, total), f32),
            jax.ShapeDtypeStruct((tok, heads * HD), bf16),
            jax.ShapeDtypeStruct((tok, 2 * HD), bf16),
        ),
        grid=(2,),
        in_specs=in_pieces_of(count, own, width)
        + [
            whole((1, width)),
            whole((width, total)),
            whole((2, HD)),
            row_block(HD // 2),
            row_block(HD // 2),
        ],
        out_specs=(row_block(width), row_block(total), row_block(heads * HD), row_block(2 * HD)),
        scratch_shapes=[pltpu.VMEM((tok, width), bf16)],
        compiler_params=pltpu.CompilerParams(vmem_limit_bytes=60 * MIB),
        cost_estimate=small_cost(2 * tok * width * total),
        name="project",
    )(*pieces, gain, bundle, head_gains, cosine, sine)


def attend(queries, tails, own_kv, low_bound, high_bound, key_place, bundle, count):
    tok, total = queries.shape
    heads = total // HD
    width = bundle.shape[0]
    span = 2 * tok
    rows = tok // 2
    first = heads + 2

    def kernel(q_ref, t_ref, o_ref, lo_ref, hi_ref, kp_ref, w_ref, att_ref, *rest):
        piece_refs, (kv, acc) = rest[:count], rest[count:]
        step, head = pl.program_id(0), pl.program_id(1)

        @pl.when((step == 0) & (head == 0))
        def _():
            kv[:tok, :] = t_ref[...]
            kv[tok:, :] = o_ref[...]

        scores = against(q_ref[...], kv[:, :HD])
        kp = kp_ref[...]
        allowed = (kp >= lo_ref[...]) & (kp <= hi_ref[...])
        masked = jnp.where(allowed, scores, masked_value)
        raised = jnp.exp(masked - jnp.max(masked, axis=1, keepdims=True))
        inverse = 1.0 / jnp.sum(raised, axis=1, keepdims=True)
        attended = product((raised * inverse).astype(bf16), kv[:, HD:], bf16)
        att_ref[...] = attended
        part = against(attended, w_ref[...])

        @pl.when(head == 0)
        def _():
            acc[...] = part

        @pl.when(head > 0)
        def _():
            acc[...] += part

        @pl.when(head == heads - 1)
        def _():
            give_rows(step, acc[...], piece_refs)

    result = pl.pallas_call(
        kernel,
        out_shape=[jax.ShapeDtypeStruct((tok, total), bf16)]
        + [jax.ShapeDtypeStruct((tok // count, width), bf16)] * count,
        grid=(2, heads),
        in_specs=[
            pl.BlockSpec((rows, HD), lambda i, h: (i, h)),
            whole((tok, 2 * HD)),
            whole((tok, 2 * HD)),
            pl.BlockSpec((rows, 1), lambda i, h: (i, 0)),
            pl.BlockSpec((rows, 1), lambda i, h: (i, 0)),
            whole((1, span)),
            pl.BlockSpec((width, HD), lambda i, h: (0, first + h)),
        ],
        out_specs=[pl.BlockSpec((rows, HD), lambda i, h: (i, h))]
        + [pl.BlockSpec((tok // count, width), lambda i, h: (0, 0))] * count,
        scratch_shapes=[pltpu.VMEM((span, 2 * HD), bf16), pltpu.VMEM((rows, width), f32)],
        compiler_params=pltpu.CompilerParams(vmem_limit_bytes=60 * MIB),
        cost_estimate=small_cost(4 * tok * span * total),
        name="attend",
    )(
        queries,
        tails,
        own_kv,
        low_bound[:, None],
        high_bound[:, None],
        key_place[None, :],
        bundle,
    )
    return result[0], result[1:]


def attend_back(queries, tails, own_kv, pieces, low_bound, high_bound, key_place, bundle):
    tok, total = queries.shape
    heads = total // HD
    count = len(pieces)
    own, width = pieces[0].shape
    span = 2 * tok
    rows = tok // 2
    first = heads + 2

    def kernel(q_ref, t_ref, o_ref, lo_ref, hi_ref, kp_ref, w_ref, *rest):
        piece_refs = rest[:count]
        dq_ref, own_ref, halo_ref, kv, full, acc = rest[count:]
        head, step = pl.program_id(0), pl.program_id(1)
        begin = (head == 0) & (step == 0)

        @pl.when(begin)
        def _():
            kv[:tok, :] = t_ref[...]
            kv[tok:, :] = o_ref[...]
            gather_rows(piece_refs, full)

        here = pl.ds(pl.multiple_of(step * rows, rows), rows)
        g = product(full[here, :], w_ref[...], bf16)
        q, k, v = q_ref[...], kv[:, :HD], kv[:, HD:]
        scores = against(k, q)
        kp = kp_ref[...]
        allowed = (kp >= lo_ref[...]) & (kp <= hi_ref[...])
        masked = jnp.where(allowed, scores, masked_value)
        raised = jnp.exp(masked - jnp.max(masked, axis=0, keepdims=True))
        probs = raised * (1.0 / jnp.sum(raised, axis=0, keepdims=True))
        prob_grad = against(v, g)
        centre = jnp.sum(probs * prob_grad, axis=0, keepdims=True)
        score_grad = (probs * (prob_grad - centre)).astype(bf16)
        dq_ref[...] = across(score_grad, k)
        dk_part = product(score_grad, q)
        dv_part = product(probs.astype(bf16), g)

        @pl.when(begin)
        def _():
            acc[:, :HD] = dk_part
            acc[:, HD:] = dv_part

        @pl.when(jnp.logical_not(begin))
        def _():
            acc[:, :HD] += dk_part
            acc[:, HD:] += dv_part

        @pl.when((head == heads - 1) & (step == 1))
        def _():
            halo_ref[...] = acc[:tok, :].astype(bf16)
            own_ref[...] = acc[tok:, :]

    return pl.pallas_call(
        kernel,
        out_shape=(
            jax.ShapeDtypeStruct((tok, total), f32),
            jax.ShapeDtypeStruct((tok, 2 * HD), f32),
            jax.ShapeDtypeStruct((tok, 2 * HD), bf16),
        ),
        grid=(heads, 2),
        in_specs=[
            pl.BlockSpec((rows, HD), lambda h, i: (i, h)),
            whole((tok, 2 * HD)),
            whole((tok, 2 * HD)),
            pl.BlockSpec((1, rows), lambda h, i: (0, i)),
            pl.BlockSpec((1, rows), lambda h, i: (0, i)),
            whole((span, 1)),
            pl.BlockSpec((width, HD), lambda h, i: (0, first + h)),
        ]
        + in_pieces_of(count, own, width),
        out_specs=(
            pl.BlockSpec((rows, HD), lambda h, i: (i, h)),
            pl.BlockSpec((tok, 2 * HD), lambda h, i: (0, 0)),
            pl.BlockSpec((tok, 2 * HD), lambda h, i: (0, 0)),
        ),
        scratch_shapes=[
            pltpu.VMEM((span, 2 * HD), bf16),
            pltpu.VMEM((tok, width), bf16),
            pltpu.VMEM((span, 2 * HD), f32),
        ],
        compiler_params=pltpu.CompilerParams(vmem_limit_bytes=60 * MIB),
        cost_estimate=small_cost(10 * tok * span * total),
        name="attend_back",
    )(
        queries,
        tails,
        own_kv,
        low_bound[None, :],
        high_bound[None, :],
        key_place[:, None],
        bundle,
        *pieces,
    )


def project_back(query_grad, own_grad, next_grad, raw, head_gains, cosine, sine, bundle, count):
    tok, total = raw.shape
    heads = query_grad.shape[1] // HD
    width = bundle.shape[0]
    rows = tok // 2

    def kernel(dq_ref, o_ref, n_ref, raw_ref, hg_ref, c_ref, s_ref, w_ref, low_ref, hg_out, *pieces):
        step = pl.program_id(0)
        cosine, sine = c_ref[...], s_ref[...]
        both = o_ref[...] + n_ref[...].astype(f32)
        raw_rows = raw_ref[...]

        def norm_back(grad, values, gain):
            scale = mean_scale(values)
            weighted = grad if gain is None else grad * gain
            centre = jnp.mean(weighted * values, axis=1, keepdims=True)
            back = scale * weighted - values * (scale * scale * scale * centre)
            return back, jnp.sum(grad * values * scale, axis=0, keepdims=True)

        gain_grad = jnp.zeros((1, HD), f32)
        for head in range(heads):
            columns = slice(head * HD, (head + 1) * HD)
            grad = turned(dq_ref[:, columns], cosine, -sine)
            back, part = norm_back(grad, raw_rows[:, columns], hg_ref[0:1, :])
            low_ref[:, columns] = back.astype(bf16)
            gain_grad = gain_grad + part
        columns = slice(heads * HD, (heads + 1) * HD)
        grad = turned(both[:, :HD], cosine, -sine)
        back, key_gain = norm_back(grad, raw_rows[:, columns], hg_ref[1:2, :])
        low_ref[:, columns] = back.astype(bf16)
        columns = slice((heads + 1) * HD, (heads + 2) * HD)
        back, _ = norm_back(both[:, HD:], raw_rows[:, columns], None)
        low_ref[:, columns] = back.astype(bf16)

        @pl.when(step == 0)
        def _():
            hg_out[0:1, :] = gain_grad
            hg_out[1:2, :] = key_gain

        @pl.when(step > 0)
        def _():
            hg_out[0:1, :] += gain_grad
            hg_out[1:2, :] += key_gain

        give_rows(step, against(low_ref[...], w_ref[...]), pieces)

    def row_block(columns):
        return pl.BlockSpec((rows, columns), lambda i: (i, 0))

    result = pl.pallas_call(
        kernel,
        out_shape=[
            jax.ShapeDtypeStruct((tok, total), bf16),
            jax.ShapeDtypeStruct((2, HD), f32),
        ]
        + [jax.ShapeDtypeStruct((tok // count, width), bf16)] * count,
        grid=(2,),
        in_specs=[
            row_block(heads * HD),
            row_block(2 * HD),
            row_block(2 * HD),
            row_block(total),
            whole((2, HD)),
            row_block(HD // 2),
            row_block(HD // 2),
            whole((width, total)),
        ],
        out_specs=[row_block(total), pl.BlockSpec((2, HD), lambda i: (0, 0))]
        + [pl.BlockSpec((tok // count, width), lambda i: (0, 0))] * count,
        compiler_params=pltpu.CompilerParams(vmem_limit_bytes=60 * MIB),
        cost_estimate=small_cost(2 * tok * width * total),
        name="project_back",
    )(query_grad, own_grad, next_grad, raw, head_gains, cosine, sine, bundle)
    return result[0], result[1], result[2:]


def feed_forward(pieces, w_ff, units):
    count = len(pieces)
    own, width = pieces[0].shape
    tok = count * own
    blk = 512

    def kernel(*refs):
        piece_refs = refs[:count]
        g_ref, u_ref, d_ref, gate_ref, up_ref, hid_ref = refs[count : count + 6]
        out_refs, (full, acc) = refs[count + 6 : 2 * count + 6], refs[2 * count + 6 :]
        step = pl.program_id(0)

        @pl.when(step == 0)
        def _():
            gather_rows(piece_refs, full)

        mid_rows = full[...]
        gate = product(mid_rows, g_ref[...])
        up = product(mid_rows, u_ref[...])
        hidden = glu_pair(gate, up).astype(bf16)
        gate_ref[...] = gate.astype(bf16)
        up_ref[...] = up.astype(bf16)
        hid_ref[...] = hidden
        part = against(hidden, d_ref[...])

        @pl.when(step == 0)
        def _():
            acc[...] = part

        @pl.when(step > 0)
        def _():
            acc[...] += part

        @pl.when(step == pl.num_programs(0) - 1)
        def _():
            for index, piece in enumerate(out_refs):
                piece[...] = acc[index * own : (index + 1) * own, :].astype(bf16)

    plane = lambda k: pl.BlockSpec((width, blk), lambda j: (0, k * (units // blk) + j))
    columns = pl.BlockSpec((tok, blk), lambda j: (0, j))
    result = pl.pallas_call(
        kernel,
        out_shape=[jax.ShapeDtypeStruct((tok, units), bf16)] * 3
        + [jax.ShapeDtypeStruct((own, width), bf16)] * count,
        grid=(units // blk,),
        in_specs=in_pieces_of(count, own, width) + [plane(0), plane(1), plane(2)],
        out_specs=[columns] * 3 + [pl.BlockSpec((own, width), lambda j: (0, 0))] * count,
        scratch_shapes=[pltpu.VMEM((tok, width), bf16), pltpu.VMEM((tok, width), f32)],
        compiler_params=pltpu.CompilerParams(vmem_limit_bytes=60 * MIB),
        cost_estimate=small_cost(6 * tok * width * units),
        name="feed_forward",
    )(*pieces, w_ff, w_ff, w_ff)
    return result[0], result[1], result[2], result[3:]


def feed_back(pieces, w_ff, gate_raw, upward):
    count = len(pieces)
    own, width = pieces[0].shape
    tok = count * own
    units = upward.shape[1]
    blk = 512

    def kernel(*refs):
        piece_refs = refs[:count]
        g_ref, u_ref, d_ref, gate_ref, up_ref, low_g_ref, low_u_ref = refs[count : count + 7]
        out_refs, (full, acc) = refs[count + 7 : 2 * count + 7], refs[2 * count + 7 :]
        step = pl.program_id(0)

        @pl.when(step == 0)
        def _():
            gather_rows(piece_refs, full)

        hidden_grad = product(full[...], d_ref[...])
        gate = gate_ref[...].astype(f32)
        _, back_glu = jax.vjp(glu_pair, gate, up_ref[...].astype(f32))
        gate_grad, up_grad = back_glu(hidden_grad)
        low_gate, low_up = gate_grad.astype(bf16), up_grad.astype(bf16)
        low_g_ref[...] = low_gate
        low_u_ref[...] = low_up
        part = against(low_gate, g_ref[...]) + against(low_up, u_ref[...])

        @pl.when(step == 0)
        def _():
            acc[...] = part

        @pl.when(step > 0)
        def _():
            acc[...] += part

        @pl.when(step == pl.num_programs(0) - 1)
        def _():
            for index, piece in enumerate(out_refs):
                piece[...] = acc[index * own : (index + 1) * own, :].astype(bf16)

    plane = lambda k: pl.BlockSpec((width, blk), lambda j: (0, k * (units // blk) + j))
    columns = pl.BlockSpec((tok, blk), lambda j: (0, j))
    result = pl.pallas_call(
        kernel,
        out_shape=[jax.ShapeDtypeStruct((tok, units), bf16)] * 2
        + [jax.ShapeDtypeStruct((own, width), bf16)] * count,
        grid=(units // blk,),
        in_specs=in_pieces_of(count, own, width)
        + [plane(0), plane(1), plane(2), columns, columns],
        out_specs=[columns] * 2
        + [pl.BlockSpec((own, width), lambda j: (0, 0))] * count,
        scratch_shapes=[pltpu.VMEM((tok, width), bf16), pltpu.VMEM((tok, width), f32)],
        compiler_params=pltpu.CompilerParams(vmem_limit_bytes=60 * MIB),
        cost_estimate=small_cost(6 * tok * width * units),
        name="feed_back",
    )(*pieces, w_ff, w_ff, w_ff, gate_raw, upward)
    return result[0], result[1], result[2:]


def column_grads(products, others, name, blk, every, parity, added=None):
    width = products[0][0][0].shape[1]
    operands, specs = [], []
    for left, right in products:
        operands += [*left, right]
        specs += [
            pl.BlockSpec((piece.shape[0], blk), lambda i, par: (0, every * i + par[0]))
            for piece in left
        ]
        specs.append(whole(right.shape))
    operands += others
    specs += [
        pl.BlockSpec((blk, other.shape[1]), lambda i, par: (every * i + par[0], 0))
        for other in others
    ]
    total = sum(mat.shape[1] for _, mat in products) + sum(other.shape[1] for other in others)
    counts = [len(left) for left, _ in products]
    out_spec = pl.BlockSpec((blk, total), lambda i, par: (i, 0))
    if added is not None:
        operands.append(added)
        specs.append(out_spec)

    def kernel(par_ref, *refs):
        o_ref, refs = refs[-1], list(refs[:-1])
        a_ref = refs.pop() if added is not None else None

        def give(value, place):
            columns = slice(place, place + value.shape[1])
            if a_ref is not None:
                value = value.astype(f32) + a_ref[:, columns].astype(f32)
            o_ref[:, columns] = value.astype(bf16)
            return columns.stop

        place = 0
        for count in counts:
            rows = jnp.concatenate([ref[...] for ref in refs[:count]], axis=0)
            place = give(across(rows, refs[count][...]), place)
            refs = refs[count + 1 :]
        for ref in refs:
            place = give(ref[...], place)

    return pl.pallas_call(
        kernel,
        out_shape=jax.ShapeDtypeStruct((width // every, total), bf16),
        grid_spec=pltpu.PrefetchScalarGridSpec(
            num_scalar_prefetch=1,
            grid=(width // blk // every,),
            in_specs=specs,
            out_specs=out_spec,
        ),
        compiler_params=pltpu.CompilerParams(vmem_limit_bytes=60 * MIB),
        cost_estimate=small_cost(1024),
        name=name,
    )(parity.reshape(1), *operands)


def crossed(piece, axis, bit):
    length = lax.axis_size(axis)
    return lax.ppermute(piece, axis, [(i, i ^ bit) for i in range(length)])


def spread_start(piece, axis):
    held = {0: piece}
    bit = lax.axis_size(axis) // 2
    while bit:
        held.update({k | bit: crossed(held[k], axis, bit) for k in list(held)})
        bit //= 2
    return [held[k] for k in range(1, len(held))]


def fold_start(chunks, axis):
    terms = {k: [chunk] for k, chunk in enumerate(chunks)}
    bit = 1
    while bit < len(chunks):
        for k in [k for k in terms if k & bit]:
            going = terms.pop(k)
            going = going[0] if len(going) == 1 else summed(going).astype(bf16)
            terms[k ^ bit].append(crossed(going, axis, bit))
        bit *= 2
    return terms[0]


def folded(chunks, axis):
    return summed(fold_start(chunks, axis))


def with_work(arrived, work):
    return lax.optimization_barrier((arrived, work))


def passed_along(shard, axis, by):
    length = lax.axis_size(axis)
    pairs = [(i, i + by) for i in range(length) if 0 <= i + by < length]
    return lax.ppermute(shard, axis, pairs)


def summed(terms):
    total = terms[0].astype(f32)
    for term in terms[1:]:
        total = total + term.astype(f32)
    return total


def rank_among(keys_own):
    count = keys_own.shape[0]
    place = jnp.arange(count, dtype=jnp.int32)
    same = (keys_own[None, :] == keys_own[:, None]) & (place[None, :] < place[:, None])
    return jnp.sum(same.astype(jnp.int32), axis=1)


def plan(lengths, order, micro, block_rows):
    devices = lax.axis_size("dp")
    parts = lax.axis_size("tensor")
    me = lax.axis_index("dp")
    part = lax.axis_index("tensor")
    tok = micro * block_rows
    own = tok // parts
    stretch = devices * block_rows
    seqs = lengths.shape[0]
    given_len = jnp.take(lengths, order)
    given_start = jnp.cumsum(given_len) - given_len
    dealt_start = jnp.cumsum(lengths) - lengths
    seq_ids = jnp.arange(seqs, dtype=jnp.int32)
    shift_given = jnp.take(dealt_start, order) - given_start
    pieces = tok // LMIN + 2
    runs = tok // stretch + 1
    per_piece = block_rows * (-(-tok // stretch)) + (parts - 1) * runs
    capacity = -(-(pieces * (per_piece // parts) + 1) // 8) * 8
    kept = -(-(tok // parts + seqs + 1) // 8) * 8

    def pick(table, index):
        return jnp.sum(jnp.where(index[:, None] == seq_ids[None, :], table[None, :], 0), axis=1)

    local = jnp.arange(tok, dtype=jnp.int32)
    stream = local // block_rows * stretch + me * block_rows + local % block_rows
    arrival = jnp.sum((stream[:, None] >= given_start[None, 1:]).astype(jnp.int32), axis=1)
    dealt = stream + pick(shift_given, arrival)
    target = dealt // tok
    quarter = dealt % parts
    send_slot = target * capacity + rank_among(target * parts + quarter)
    send_slot = jnp.where(quarter == part, send_slot, -1)
    keep_rank = rank_among(quarter)
    keep_slot = (part ^ quarter) * kept + keep_rank

    place = me * tok + jnp.arange(own, dtype=jnp.int32) * parts + part
    own_seq = jnp.sum((place[:, None] >= dealt_start[None, 1:]).astype(jnp.int32), axis=1)
    shift_dealt = jnp.sum(
        jnp.where(order[None, :] == seq_ids[:, None], -shift_given[None, :], 0), axis=1
    )
    anchor = place + pick(shift_dealt, own_seq)
    source = anchor % stretch // block_rows
    prior = (anchor[None, :] < anchor[:, None]) & (source[None, :] == source[:, None])
    recv_slot = source * capacity + jnp.sum(prior.astype(jnp.int32), axis=1)

    total = devices * capacity
    slots = jnp.arange(total, dtype=jnp.int32)
    sender = (slots[:, None] == send_slot[None, :]).astype(bf16)
    receiver = (recv_slot[:, None] == slots[None, :]).astype(bf16)
    mine = jnp.where(quarter == part, keep_rank, -1)
    chosen = (jnp.arange(kept, dtype=jnp.int32)[:, None] == mine[None, :]).astype(bf16)
    compact = against(chosen, sender, bf16)
    homing = (
        keep_slot[:, None] == jnp.arange(parts * kept, dtype=jnp.int32)[None, :]
    ).astype(bf16)

    held = part ^ jnp.arange(parts, dtype=jnp.int32)
    rows = (jnp.arange(own, dtype=jnp.int32)[None, :] * parts + held[:, None]).reshape(tok)
    both = me * tok + jnp.concatenate([rows - tok, rows])
    ext_seq = jnp.sum((both[:, None] >= dealt_start[None, 1:]).astype(jnp.int32), axis=1)
    start = pick(dealt_start, ext_seq[tok:])
    high_bound = both[tok:]
    low_bound = jnp.maximum(start, high_bound - (WIN - 1))
    return sender, receiver, compact, homing, (low_bound, high_bound, both), high_bound - start


def body(
    hidden_in,
    layer_inputs,
    out_grad,
    lengths,
    order,
    w_query,
    w_keyval,
    w_out,
    w_left,
    w_right,
    w_gateup,
    w_down,
    w_pergate,
    w_perproj,
    gains,
    head_gains,
):
    devices = lax.axis_size("dp")
    me = lax.axis_index("dp")
    parts = lax.axis_size("tensor")
    part = lax.axis_index("tensor")
    micro, block_rows, width = hidden_in.shape
    per_width = layer_inputs.shape[2]
    tok = micro * block_rows
    assert tok == WIN
    sender, receiver, compact, homing, bounds, own_pos = plan(lengths, order, micro, block_rows)

    kv_cols = part // (parts // KVH) * HD
    kv_own = lax.dynamic_slice_in_dim(w_keyval, kv_cols, HD, 2)
    gains_high = lax.reduce_precision(gains, 8, 7)
    gains_low = (gains - gains_high).astype(bf16)
    gain_cols = jnp.concatenate([gains_high.astype(bf16), gains_low], axis=0)
    gain_cols = jnp.pad(gain_cols, ((0, LANES - gain_cols.shape[0]), (0, 0))).T
    q_width = w_query.shape[1]
    rank = w_left.shape[1]

    def gather_columns(pieces):
        marks = [0]
        for piece in pieces:
            marks.append(marks[-1] + piece.shape[1])
        full = lax.all_gather(jnp.concatenate(pieces, axis=1), "dp", axis=0, tiled=True)
        return full, [full[:, a:b] for a, b in zip(marks[:-1], marks[1:])]

    first = [w_query, kv_own[0], kv_own[1], w_out.T, w_left, w_right.T, gain_cols]
    bundle_a, (wq, wk, wv, wo_t, wl, wr_t, gain_f) = gather_columns(first)
    units = w_down.shape[0]
    flat = jnp.concatenate(
        [
            hidden_in.reshape(tok, width),
            layer_inputs.reshape(tok, per_width),
            out_grad.reshape(tok, width),
        ],
        axis=1,
    )
    packed = product(sender, flat, bf16)
    first_cols = width + per_width
    come_in = lax.all_to_all(packed[:, :width], "dp", 0, 0, tiled=True)
    low_inputs = product(receiver, come_in, bf16)
    inputs = low_inputs.astype(f32)
    token_pieces = spread_start(low_inputs, "tensor")
    second = [w_gateup[0], w_gateup[1], w_down.T, w_pergate, w_perproj.T]
    w_ff, (_, _, _, wg, wp_t) = gather_columns(second)
    w_gains = gain_f.T
    gains_f = w_gains[:6].astype(f32) + w_gains[6:12].astype(f32)
    angles = own_pos.astype(f32)[:, None] * frequencies()

    def homeward(rows_own):
        return lax.all_to_all(across(receiver, rows_own, bf16), "dp", 0, 0, tiled=True)

    block = width // devices
    paired = devices > 1 and block % (2 * LANES) == 0
    low_bit = me % 2
    groups = [list(range(k, devices, 2)) for k in range(2)] if paired else None

    def scattered(grads, swap):
        return lax.psum_scatter(
            grads,
            "dp",
            scatter_dimension=0,
            axis_index_groups=groups if swap else None,
            tiled=True,
        )

    def grads_beside_fold(chunks, products, others, name, swap):
        def make(*where):
            return column_grads(products, others, name, *where)

        if not (paired and swap):
            return fold_start(chunks, "tensor"), make(2 * LANES, 1, jnp.zeros((), jnp.int32))
        leaving = make(block, 2, 1 - low_bit)
        chunks, leaving = with_work(chunks, leaving)
        pieces = fold_start(chunks, "tensor")
        return pieces, make(block, 2, low_bit, crossed(leaving, "dp", 1))

    cosine, sine = jnp.cos(angles), jnp.sin(angles)
    heads = q_width // HD
    all_in, raw, queries, own_kv = project(
        [low_inputs] + token_pieces, gains_f[:1], bundle_a, head_gains, cosine, sine, heads
    )
    normal_in = normed(inputs, gains_f[0])
    low_in = normal_in.astype(bf16)
    tails = passed_along(own_kv, "dp", 1)
    low_att, branch_parts = attend(queries, tails, own_kv, *bounds, bundle_a, parts)
    branch = folded(branch_parts, "tensor")

    low_rank = product(low_in, wl, bf16)
    laurel_raw = against(low_rank, wr_t)
    first_sum = (
        inputs + normed(branch, gains_f[1]) + normal_in + normed(laurel_raw, gains_f[2])
    ) * half_root
    low_mid = normed(first_sum, gains_f[3]).astype(bf16)

    all_mid = [low_mid] + spread_start(low_mid, "tensor")
    rest_out, w_ff = with_work(packed[:, width:], w_ff)
    come_rest = lax.all_to_all(rest_out, "dp", 0, 0, tiled=True)
    gate_raw, upward, low_hidden, feed_parts = feed_forward(all_mid, w_ff, units)
    feed_parts, come_rest = with_work(feed_parts, come_rest)
    fed_pieces = fold_start(feed_parts, "tensor")
    rest = product(receiver, come_rest, bf16)
    layer_in = rest[:, :per_width].astype(f32)
    cotangent = rest[:, per_width:].astype(f32)
    feed_raw = summed(fed_pieces)

    second_sum = first_sum + normed(feed_raw, gains_f[4])
    low_second = second_sum.astype(bf16)
    pre_gate = product(low_second, wg)
    low_gated = (gelu_tanh(pre_gate) * layer_in).astype(bf16)
    per_raw = against(low_gated, wp_t)
    result = second_sum + normed(per_raw, gains_f[5])

    _, back_per = jax.vjp(normed, per_raw, gains_f[5])
    per_grad, grad_g5 = back_per(cotangent)
    low_per = per_grad.astype(bf16)
    gated_grad = product(low_per, wp_t)
    gelu_out, back_gelu = jax.vjp(gelu_tanh, pre_gate)
    low_pre = back_gelu(gated_grad * layer_in)[0].astype(bf16)
    layer_grad = gated_grad * gelu_out
    second_grad = cotangent + against(low_pre, wg)
    _, back_feed = jax.vjp(normed, feed_raw, gains_f[4])
    feed_grad, grad_g4 = back_feed(second_grad)
    low_feed = feed_grad.astype(bf16)

    feed_pieces = spread_start(low_feed, "tensor")
    grad_perproj = across(low_per, low_gated, bf16)
    grad_pergate = across(low_second, low_pre, bf16)
    low_result = jnp.concatenate([result.astype(bf16), layer_grad.astype(bf16)], axis=1)
    come_one = homeward(low_result)
    feed_pieces, (grad_perproj, grad_pergate, come_one) = with_work(
        feed_pieces, (grad_perproj, grad_pergate, come_one)
    )
    all_feed = [low_feed] + feed_pieces

    home_one = product(compact, come_one, bf16)
    home_pieces = spread_start(home_one, "tensor")
    low_gate, low_up, mid_parts = feed_back(all_feed, w_ff, gate_raw, upward)
    mid_parts, home_pieces[0] = with_work(mid_parts, home_pieces[0])
    mid_parts, home_pieces[1] = with_work(mid_parts, home_pieces[1])

    mid_pieces, ff_grads = grads_beside_fold(
        mid_parts,
        [(all_mid, low_gate), (all_mid, low_up), (all_feed, low_hidden)],
        [grad_pergate, grad_perproj],
        "feed_grads",
        False,
    )
    mid_pieces, ff_grads = with_work(mid_pieces, ff_grads)
    s_ff = scattered(ff_grads, False)
    mid_grad = summed(mid_pieces)

    _, back_mid = jax.vjp(normed, first_sum, gains_f[3])
    first_part, grad_g3 = back_mid(mid_grad)
    shared = (second_grad + first_part) * half_root
    _, back_laurel = jax.vjp(normed, laurel_raw, gains_f[2])
    laurel_grad, grad_g2 = back_laurel(shared)
    low_laurel = laurel_grad.astype(bf16)
    _, back_branch = jax.vjp(normed, branch, gains_f[1])
    branch_grad, grad_g1 = back_branch(shared)
    low_branch = branch_grad.astype(bf16)

    branch_pieces = spread_start(low_branch, "tensor")
    low_rank_grad = product(low_laurel, wr_t, bf16)
    grad_right = across(low_laurel, low_rank, bf16)
    grad_left = across(low_in, low_rank_grad, bf16)
    small = jnp.concatenate([grad_left, grad_right], axis=1)
    gain_part = jnp.stack([grad_g1, grad_g2, grad_g3, grad_g4, grad_g5])
    branch_pieces, (small, gain_part) = with_work(branch_pieces, (small, gain_part))
    all_branch = [low_branch] + branch_pieces

    query_grad, own_grad, halo_grad = attend_back(
        queries, tails, own_kv, all_branch, *bounds, bundle_a
    )
    query_grad, home_pieces[-1] = with_work(query_grad, home_pieces[-1])
    next_grad = passed_along(halo_grad, "dp", -1)
    low_qkv, head_grads, in_parts = project_back(
        query_grad, own_grad, next_grad, raw, head_gains, cosine, sine, bundle_a, parts
    )

    head_cols = head_grads.reshape(-1, width // devices)
    head_count = head_cols.shape[0]
    head_cols = jnp.tile(head_cols, (1, devices))
    last_cols = jnp.concatenate([gain_part, head_cols], axis=0).astype(bf16)
    last_cols = jnp.pad(last_cols, ((0, LANES - last_cols.shape[0]), (0, 0))).T
    in_pieces, at_grads = grads_beside_fold(
        in_parts,
        [([all_in], low_qkv), (all_branch, low_att)],
        [small, last_cols],
        "attention_grads",
        True,
    )
    in_pieces, at_grads = with_work(in_pieces, at_grads)
    in_attn = summed(in_pieces)
    normal_grad = in_attn + against(low_rank_grad, wl) + shared
    _, back_in = jax.vjp(normed, inputs, gains_f[0])
    in_part, grad_g0 = back_in(normal_grad)
    input_grad = shared + in_part
    extra = jnp.pad(
        grad_g0.reshape(devices, 1, block),
        ((0, 0), (receiver.shape[1] // devices - 1, 0), (0, width - block)),
    )
    sent_two = across(receiver, input_grad.astype(bf16)) + extra.reshape(-1, width)
    come_two = lax.all_to_all(sent_two.astype(bf16), "dp", 0, 0, tiled=True)
    at_grads, (s_ff, come_two) = with_work(at_grads, (s_ff, come_two))
    s_at = scattered(at_grads, True)
    early = s_ff[:, 3 * units :]
    bit = 1
    while bit < parts:
        early = summed([early, crossed(early, "tensor", bit)])
        early = early.astype(bf16) if 2 * bit < parts else early
        bit *= 2
    g0_part = jnp.sum(come_two.reshape(devices, -1, width)[:, -1, :block].astype(f32), axis=0)
    home_two = product(compact, come_two) + jnp.pad(
        g0_part[None], ((compact.shape[0] - 1, 0), (0, width - block))
    )
    home_two = home_two.astype(bf16)
    all_two = jnp.concatenate([home_two] + spread_start(home_two, "tensor"), axis=0)
    back_two = product(homing, all_two, bf16)
    g0_terms = all_two.reshape(parts, -1, width)[:, -1, :block].astype(f32)
    while g0_terms.shape[0] > 1:
        middle = g0_terms.shape[0] // 2
        g0_terms = g0_terms[:middle] + g0_terms[middle:]

    shard_gateup = jnp.stack([s_ff[:, :units], s_ff[:, units : 2 * units]]).astype(f32)
    shard_down = s_ff[:, 2 * units : 3 * units].T.astype(f32)
    o_kv = q_width + 2 * HD
    o_small = o_kv + w_out.shape[0]
    shard_query = s_at[:, :q_width].astype(f32)
    shard_out = s_at[:, o_kv:o_small].T.astype(f32)
    kv_cols = 2 * HD
    exchanged = jnp.concatenate([s_at[:, q_width:o_kv], s_at[:, o_small:]], axis=1)
    bit = 1
    while bit < parts // KVH:
        exchanged = summed([exchanged, crossed(exchanged, "tensor", bit)]).astype(bf16)
        bit *= 2
    arrived = crossed(exchanged, "tensor", bit)
    kv_sum, kv_other = exchanged[:, :kv_cols], arrived[:, :kv_cols]
    small_sum = summed([exchanged[:, kv_cols:], arrived[:, kv_cols:]])
    shard_left = small_sum[:, :rank]
    shard_right = small_sum[:, rank : 2 * rank].T
    shard_pergate = early[:, :per_width]
    shard_perproj = early[:, per_width:].T
    last_sum = small_sum[:, 2 * rank :].T
    shard_gains = jnp.concatenate([g0_terms, last_sum[:5]], axis=0)
    head_total = last_sum[5 : 5 + head_count].reshape(2, HD)
    upper = part // (parts // KVH) == 1
    low_head = jnp.where(upper, kv_other, kv_sum).astype(f32)
    high_head = jnp.where(upper, kv_sum, kv_other).astype(f32)
    shard_keyval = jnp.stack(
        [
            jnp.concatenate([low_head[:, :HD], high_head[:, :HD]], axis=1),
            jnp.concatenate([low_head[:, HD:], high_head[:, HD:]], axis=1),
        ]
    )
    back_one = product(homing, jnp.concatenate([home_one] + home_pieces, axis=0), bf16)
    return (
        back_one[:, :width].reshape(micro, block_rows, width),
        back_two.reshape(micro, block_rows, width),
        back_one[:, width:].reshape(micro, block_rows, per_width),
        shard_query,
        shard_keyval,
        shard_out,
        shard_left,
        shard_right,
        shard_gateup,
        shard_down,
        shard_pergate,
        shard_perproj,
        shard_gains,
        head_total,
    )


def solution(mesh):
    placed = (
        P(None, "dp", None),
        P(None, "dp", None),
        P(None, "dp", None),
        P(),
        P(),
        P("dp", "tensor"),
        P(None, "dp", None),
        P("tensor", "dp"),
        P("dp", None),
        P(None, "dp"),
        P(None, "dp", "tensor"),
        P("tensor", "dp"),
        P("dp", None),
        P(None, "dp"),
        P(None, "dp"),
        P(),
    )
    return jax.shard_map(
        body,
        mesh=mesh,
        in_specs=placed,
        out_specs=(
            P(None, "dp", None),
            P(None, "dp", None),
            P(None, "dp", None),
            P("dp", "tensor"),
            P(None, "dp", None),
            P("tensor", "dp"),
            P("dp", None),
            P(None, "dp"),
            P(None, "dp", "tensor"),
            P("tensor", "dp"),
            P("dp", None),
            P(None, "dp"),
            P(None, "dp"),
            P(),
        ),
        check_vma=False,
    )
```

```python
import jax
import jax.numpy as jnp
from jax import lax
from jax.experimental import pallas as pl
from jax.experimental.pallas import tpu as pltpu
from jax.sharding import PartitionSpec as P

KVH = 2
HD = 256
WIN = 512
LMIN = 1024
LANES = 128

half_root = 0.7071067811865476
masked_value = -1e30
bf16 = jnp.bfloat16
f32 = jnp.float32


def normed(values_in, gain_vec):
    norm_scale = lax.rsqrt(jnp.mean(values_in * values_in, axis=-1, keepdims=True) + 1e-06)
    return values_in * norm_scale * gain_vec


def rotate(values_in, angles):
    half_dim = values_in.shape[-1] // 2
    first_half = values_in[..., :half_dim]
    second_half = values_in[..., half_dim:]
    cosine = jnp.cos(angles)
    sine_part = jnp.sin(angles)
    return jnp.concatenate(
        [
            first_half * cosine - second_half * sine_part,
            second_half * cosine + first_half * sine_part,
        ],
        axis=-1,
    )


def gelu_tanh(values_in):
    return jax.nn.gelu(values_in, approximate=True)


def glu_pair(gate_raw, upward):
    return gelu_tanh(gate_raw) * upward


def value_map(raw_value):
    return normed(raw_value, 1.0)


def product(left_mat, right_mat, kind=f32):
    return jnp.dot(left_mat, right_mat, preferred_element_type=f32).astype(kind)


def against(left_mat, right_mat, kind=f32):
    return lax.dot_general(
        left_mat, right_mat, (((1,), (1,)), ((), ())), preferred_element_type=f32
    ).astype(kind)


def across(left_mat, right_mat, kind=f32):
    return lax.dot_general(
        left_mat, right_mat, (((0,), (0,)), ((), ())), preferred_element_type=f32
    ).astype(kind)


def frequencies():
    half_dim = HD // 2
    return jnp.power(10000.0, -2.0 * jnp.arange(half_dim, dtype=f32) / HD)


MIB = 1 << 20


def small_cost(flops):
    return pl.CostEstimate(flops=flops, bytes_accessed=1024, transcendentals=0)


def whole(shape):
    zeros = (0,) * len(shape)
    return pl.BlockSpec(shape, lambda *_: zeros, pipeline_mode=pl.Buffered(1))


def in_pieces_of(count, rows, width):
    return [whole((rows, width)) for _ in range(count)]


def gather_rows(piece_refs, full_ref):
    rows = piece_refs[0].shape[0]
    for index, piece in enumerate(piece_refs):
        full_ref[index * rows : (index + 1) * rows, :] = piece[...]


def give_rows(step, value, piece_refs):
    rows = piece_refs[0].shape[0]
    each = value.shape[0] // rows
    for index, piece in enumerate(piece_refs):
        place = index % each * rows

        @pl.when(step == index // each)
        def _():
            piece[...] = value[place : place + rows, :].astype(bf16)


def mean_scale(values):
    return lax.rsqrt(jnp.mean(values * values, axis=1, keepdims=True) + 1e-06)


def turned(values, cosine, sine):
    half = values.shape[1] // 2
    first, second = values[:, :half], values[:, half:]
    return jnp.concatenate(
        [first * cosine - second * sine, second * cosine + first * sine], axis=1
    )


def project(pieces, gain, bundle, head_gains, cosine, sine, heads):
    count = len(pieces)
    own, width = pieces[0].shape
    tok = count * own
    total = (heads + 2) * HD
    rows = tok // 2

    def kernel(*refs):
        piece_refs = refs[:count]
        g_ref, w_ref, hg_ref, c_ref, s_ref, in_ref, raw_ref, q_ref, kv_ref, full = refs[count:]
        step = pl.program_id(0)

        @pl.when(step == 0)
        def _():
            gather_rows(piece_refs, full)

        x = full[pl.ds(pl.multiple_of(step * rows, rows), rows), :].astype(f32)
        low = (x * mean_scale(x) * g_ref[...]).astype(bf16)
        in_ref[...] = low
        raw = product(low, w_ref[...])
        raw_ref[...] = raw
        cosine, sine = c_ref[...], s_ref[...]
        for head in range(heads):
            part = raw[:, head * HD : (head + 1) * HD]
            part = part * mean_scale(part) * hg_ref[0:1, :]
            q_ref[:, head * HD : (head + 1) * HD] = turned(part, cosine, sine).astype(bf16)
        part = raw[:, heads * HD : (heads + 1) * HD]
        part = part * mean_scale(part) * hg_ref[1:2, :]
        kv_ref[:, :HD] = turned(part, cosine, sine).astype(bf16)
        part = raw[:, (heads + 1) * HD :]
        kv_ref[:, HD:] = (part * mean_scale(part)).astype(bf16)

    def row_block(columns):
        return pl.BlockSpec((rows, columns), lambda i: (i, 0))

    return pl.pallas_call(
        kernel,
        out_shape=(
            jax.ShapeDtypeStruct((tok, width), bf16),
            jax.ShapeDtypeStruct((tok, total), f32),
            jax.ShapeDtypeStruct((tok, heads * HD), bf16),
            jax.ShapeDtypeStruct((tok, 2 * HD), bf16),
        ),
        grid=(2,),
        in_specs=in_pieces_of(count, own, width)
        + [
            whole((1, width)),
            whole((width, total)),
            whole((2, HD)),
            row_block(HD // 2),
            row_block(HD // 2),
        ],
        out_specs=(row_block(width), row_block(total), row_block(heads * HD), row_block(2 * HD)),
        scratch_shapes=[pltpu.VMEM((tok, width), bf16)],
        compiler_params=pltpu.CompilerParams(vmem_limit_bytes=60 * MIB),
        cost_estimate=small_cost(2 * tok * width * total),
        name="project",
    )(*pieces, gain, bundle, head_gains, cosine, sine)


def attend(queries, tails, own_kv, low_bound, high_bound, key_place, bundle, count):
    tok, total = queries.shape
    heads = total // HD
    width = bundle.shape[0]
    span = 2 * tok
    rows = tok // 2
    first = heads + 2

    def kernel(q_ref, t_ref, o_ref, lo_ref, hi_ref, kp_ref, w_ref, att_ref, *rest):
        piece_refs, (kv, acc) = rest[:count], rest[count:]
        step, head = pl.program_id(0), pl.program_id(1)

        @pl.when((step == 0) & (head == 0))
        def _():
            kv[:tok, :] = t_ref[...]
            kv[tok:, :] = o_ref[...]

        scores = against(q_ref[...], kv[:, :HD])
        kp = kp_ref[...]
        allowed = (kp >= lo_ref[...]) & (kp <= hi_ref[...])
        masked = jnp.where(allowed, scores, masked_value)
        raised = jnp.exp(masked - jnp.max(masked, axis=1, keepdims=True))
        inverse = 1.0 / jnp.sum(raised, axis=1, keepdims=True)
        attended = product((raised * inverse).astype(bf16), kv[:, HD:], bf16)
        att_ref[...] = attended
        part = against(attended, w_ref[...])

        @pl.when(head == 0)
        def _():
            acc[...] = part

        @pl.when(head > 0)
        def _():
            acc[...] += part

        @pl.when(head == heads - 1)
        def _():
            give_rows(step, acc[...], piece_refs)

    result = pl.pallas_call(
        kernel,
        out_shape=[jax.ShapeDtypeStruct((tok, total), bf16)]
        + [jax.ShapeDtypeStruct((tok // count, width), bf16)] * count,
        grid=(2, heads),
        in_specs=[
            pl.BlockSpec((rows, HD), lambda i, h: (i, h)),
            whole((tok, 2 * HD)),
            whole((tok, 2 * HD)),
            pl.BlockSpec((rows, 1), lambda i, h: (i, 0)),
            pl.BlockSpec((rows, 1), lambda i, h: (i, 0)),
            whole((1, span)),
            pl.BlockSpec((width, HD), lambda i, h: (0, first + h)),
        ],
        out_specs=[pl.BlockSpec((rows, HD), lambda i, h: (i, h))]
        + [pl.BlockSpec((tok // count, width), lambda i, h: (0, 0))] * count,
        scratch_shapes=[pltpu.VMEM((span, 2 * HD), bf16), pltpu.VMEM((rows, width), f32)],
        compiler_params=pltpu.CompilerParams(vmem_limit_bytes=60 * MIB),
        cost_estimate=small_cost(4 * tok * span * total),
        name="attend",
    )(
        queries,
        tails,
        own_kv,
        low_bound[:, None],
        high_bound[:, None],
        key_place[None, :],
        bundle,
    )
    return result[0], result[1:]


def attend_back(queries, tails, own_kv, pieces, low_bound, high_bound, key_place, bundle):
    tok, total = queries.shape
    heads = total // HD
    count = len(pieces)
    own, width = pieces[0].shape
    span = 2 * tok
    rows = tok // 2
    first = heads + 2

    def kernel(q_ref, t_ref, o_ref, lo_ref, hi_ref, kp_ref, w_ref, *rest):
        piece_refs = rest[:count]
        dq_ref, own_ref, halo_ref, kv, full, acc = rest[count:]
        head, step = pl.program_id(0), pl.program_id(1)
        begin = (head == 0) & (step == 0)

        @pl.when(begin)
        def _():
            kv[:tok, :] = t_ref[...]
            kv[tok:, :] = o_ref[...]
            gather_rows(piece_refs, full)

        here = pl.ds(pl.multiple_of(step * rows, rows), rows)
        g = product(full[here, :], w_ref[...], bf16)
        q, k, v = q_ref[...], kv[:, :HD], kv[:, HD:]
        scores = against(k, q)
        kp = kp_ref[...]
        allowed = (kp >= lo_ref[...]) & (kp <= hi_ref[...])
        masked = jnp.where(allowed, scores, masked_value)
        raised = jnp.exp(masked - jnp.max(masked, axis=0, keepdims=True))
        probs = raised * (1.0 / jnp.sum(raised, axis=0, keepdims=True))
        prob_grad = against(v, g)
        centre = jnp.sum(probs * prob_grad, axis=0, keepdims=True)
        score_grad = (probs * (prob_grad - centre)).astype(bf16)
        dq_ref[...] = across(score_grad, k)
        dk_part = product(score_grad, q)
        dv_part = product(probs.astype(bf16), g)

        @pl.when(begin)
        def _():
            acc[:, :HD] = dk_part
            acc[:, HD:] = dv_part

        @pl.when(jnp.logical_not(begin))
        def _():
            acc[:, :HD] += dk_part
            acc[:, HD:] += dv_part

        @pl.when((head == heads - 1) & (step == 1))
        def _():
            halo_ref[...] = acc[:tok, :].astype(bf16)
            own_ref[...] = acc[tok:, :]

    return pl.pallas_call(
        kernel,
        out_shape=(
            jax.ShapeDtypeStruct((tok, total), f32),
            jax.ShapeDtypeStruct((tok, 2 * HD), f32),
            jax.ShapeDtypeStruct((tok, 2 * HD), bf16),
        ),
        grid=(heads, 2),
        in_specs=[
            pl.BlockSpec((rows, HD), lambda h, i: (i, h)),
            whole((tok, 2 * HD)),
            whole((tok, 2 * HD)),
            pl.BlockSpec((1, rows), lambda h, i: (0, i)),
            pl.BlockSpec((1, rows), lambda h, i: (0, i)),
            whole((span, 1)),
            pl.BlockSpec((width, HD), lambda h, i: (0, first + h)),
        ]
        + in_pieces_of(count, own, width),
        out_specs=(
            pl.BlockSpec((rows, HD), lambda h, i: (i, h)),
            pl.BlockSpec((tok, 2 * HD), lambda h, i: (0, 0)),
            pl.BlockSpec((tok, 2 * HD), lambda h, i: (0, 0)),
        ),
        scratch_shapes=[
            pltpu.VMEM((span, 2 * HD), bf16),
            pltpu.VMEM((tok, width), bf16),
            pltpu.VMEM((span, 2 * HD), f32),
        ],
        compiler_params=pltpu.CompilerParams(vmem_limit_bytes=60 * MIB),
        cost_estimate=small_cost(10 * tok * span * total),
        name="attend_back",
    )(
        queries,
        tails,
        own_kv,
        low_bound[None, :],
        high_bound[None, :],
        key_place[:, None],
        bundle,
        *pieces,
    )


def project_back(query_grad, own_grad, next_grad, raw, head_gains, cosine, sine, bundle, count):
    tok, total = raw.shape
    heads = query_grad.shape[1] // HD
    width = bundle.shape[0]
    rows = tok // 2

    def kernel(dq_ref, o_ref, n_ref, raw_ref, hg_ref, c_ref, s_ref, w_ref, low_ref, hg_out, *pieces):
        step = pl.program_id(0)
        cosine, sine = c_ref[...], s_ref[...]
        both = o_ref[...] + n_ref[...].astype(f32)
        raw_rows = raw_ref[...]

        def norm_back(grad, values, gain):
            scale = mean_scale(values)
            weighted = grad if gain is None else grad * gain
            centre = jnp.mean(weighted * values, axis=1, keepdims=True)
            back = scale * weighted - values * (scale * scale * scale * centre)
            return back, jnp.sum(grad * values * scale, axis=0, keepdims=True)

        gain_grad = jnp.zeros((1, HD), f32)
        for head in range(heads):
            columns = slice(head * HD, (head + 1) * HD)
            grad = turned(dq_ref[:, columns], cosine, -sine)
            back, part = norm_back(grad, raw_rows[:, columns], hg_ref[0:1, :])
            low_ref[:, columns] = back.astype(bf16)
            gain_grad = gain_grad + part
        columns = slice(heads * HD, (heads + 1) * HD)
        grad = turned(both[:, :HD], cosine, -sine)
        back, key_gain = norm_back(grad, raw_rows[:, columns], hg_ref[1:2, :])
        low_ref[:, columns] = back.astype(bf16)
        columns = slice((heads + 1) * HD, (heads + 2) * HD)
        back, _ = norm_back(both[:, HD:], raw_rows[:, columns], None)
        low_ref[:, columns] = back.astype(bf16)

        @pl.when(step == 0)
        def _():
            hg_out[0:1, :] = gain_grad
            hg_out[1:2, :] = key_gain

        @pl.when(step > 0)
        def _():
            hg_out[0:1, :] += gain_grad
            hg_out[1:2, :] += key_gain

        give_rows(step, against(low_ref[...], w_ref[...]), pieces)

    def row_block(columns):
        return pl.BlockSpec((rows, columns), lambda i: (i, 0))

    result = pl.pallas_call(
        kernel,
        out_shape=[
            jax.ShapeDtypeStruct((tok, total), bf16),
            jax.ShapeDtypeStruct((2, HD), f32),
        ]
        + [jax.ShapeDtypeStruct((tok // count, width), bf16)] * count,
        grid=(2,),
        in_specs=[
            row_block(heads * HD),
            row_block(2 * HD),
            row_block(2 * HD),
            row_block(total),
            whole((2, HD)),
            row_block(HD // 2),
            row_block(HD // 2),
            whole((width, total)),
        ],
        out_specs=[row_block(total), pl.BlockSpec((2, HD), lambda i: (0, 0))]
        + [pl.BlockSpec((tok // count, width), lambda i: (0, 0))] * count,
        compiler_params=pltpu.CompilerParams(vmem_limit_bytes=60 * MIB),
        cost_estimate=small_cost(2 * tok * width * total),
        name="project_back",
    )(query_grad, own_grad, next_grad, raw, head_gains, cosine, sine, bundle)
    return result[0], result[1], result[2:]


def feed_forward(pieces, w_ff, units):
    count = len(pieces)
    own, width = pieces[0].shape
    tok = count * own
    blk = 512

    def kernel(*refs):
        piece_refs = refs[:count]
        g_ref, u_ref, d_ref, gate_ref, up_ref, hid_ref = refs[count : count + 6]
        out_refs, (full, acc) = refs[count + 6 : 2 * count + 6], refs[2 * count + 6 :]
        step = pl.program_id(0)

        @pl.when(step == 0)
        def _():
            gather_rows(piece_refs, full)

        mid_rows = full[...]
        gate = product(mid_rows, g_ref[...])
        up = product(mid_rows, u_ref[...])
        hidden = glu_pair(gate, up).astype(bf16)
        gate_ref[...] = gate.astype(bf16)
        up_ref[...] = up.astype(bf16)
        hid_ref[...] = hidden
        part = against(hidden, d_ref[...])

        @pl.when(step == 0)
        def _():
            acc[...] = part

        @pl.when(step > 0)
        def _():
            acc[...] += part

        @pl.when(step == pl.num_programs(0) - 1)
        def _():
            for index, piece in enumerate(out_refs):
                piece[...] = acc[index * own : (index + 1) * own, :].astype(bf16)

    plane = lambda k: pl.BlockSpec((width, blk), lambda j: (0, k * (units // blk) + j))
    columns = pl.BlockSpec((tok, blk), lambda j: (0, j))
    result = pl.pallas_call(
        kernel,
        out_shape=[jax.ShapeDtypeStruct((tok, units), bf16)] * 3
        + [jax.ShapeDtypeStruct((own, width), bf16)] * count,
        grid=(units // blk,),
        in_specs=in_pieces_of(count, own, width) + [plane(0), plane(1), plane(2)],
        out_specs=[columns] * 3 + [pl.BlockSpec((own, width), lambda j: (0, 0))] * count,
        scratch_shapes=[pltpu.VMEM((tok, width), bf16), pltpu.VMEM((tok, width), f32)],
        compiler_params=pltpu.CompilerParams(vmem_limit_bytes=60 * MIB),
        cost_estimate=small_cost(6 * tok * width * units),
        name="feed_forward",
    )(*pieces, w_ff, w_ff, w_ff)
    return result[0], result[1], result[2], result[3:]


def feed_back(pieces, w_ff, gate_raw, upward):
    count = len(pieces)
    own, width = pieces[0].shape
    tok = count * own
    units = upward.shape[1]
    blk = 512

    def kernel(*refs):
        piece_refs = refs[:count]
        g_ref, u_ref, d_ref, gate_ref, up_ref, low_g_ref, low_u_ref = refs[count : count + 7]
        out_refs, (full, acc) = refs[count + 7 : 2 * count + 7], refs[2 * count + 7 :]
        step = pl.program_id(0)

        @pl.when(step == 0)
        def _():
            gather_rows(piece_refs, full)

        hidden_grad = product(full[...], d_ref[...])
        gate = gate_ref[...].astype(f32)
        _, back_glu = jax.vjp(glu_pair, gate, up_ref[...].astype(f32))
        gate_grad, up_grad = back_glu(hidden_grad)
        low_gate, low_up = gate_grad.astype(bf16), up_grad.astype(bf16)
        low_g_ref[...] = low_gate
        low_u_ref[...] = low_up
        part = against(low_gate, g_ref[...]) + against(low_up, u_ref[...])

        @pl.when(step == 0)
        def _():
            acc[...] = part

        @pl.when(step > 0)
        def _():
            acc[...] += part

        @pl.when(step == pl.num_programs(0) - 1)
        def _():
            for index, piece in enumerate(out_refs):
                piece[...] = acc[index * own : (index + 1) * own, :].astype(bf16)

    plane = lambda k: pl.BlockSpec((width, blk), lambda j: (0, k * (units // blk) + j))
    columns = pl.BlockSpec((tok, blk), lambda j: (0, j))
    result = pl.pallas_call(
        kernel,
        out_shape=[jax.ShapeDtypeStruct((tok, units), bf16)] * 2
        + [jax.ShapeDtypeStruct((own, width), bf16)] * count,
        grid=(units // blk,),
        in_specs=in_pieces_of(count, own, width)
        + [plane(0), plane(1), plane(2), columns, columns],
        out_specs=[columns] * 2
        + [pl.BlockSpec((own, width), lambda j: (0, 0))] * count,
        scratch_shapes=[pltpu.VMEM((tok, width), bf16), pltpu.VMEM((tok, width), f32)],
        compiler_params=pltpu.CompilerParams(vmem_limit_bytes=60 * MIB),
        cost_estimate=small_cost(6 * tok * width * units),
        name="feed_back",
    )(*pieces, w_ff, w_ff, w_ff, gate_raw, upward)
    return result[0], result[1], result[2:]


def column_grads(products, others, name, blk, every, parity, added=None):
    width = products[0][0][0].shape[1]
    operands, specs = [], []
    for left, right in products:
        operands += [*left, right]
        specs += [
            pl.BlockSpec((piece.shape[0], blk), lambda i, par: (0, every * i + par[0]))
            for piece in left
        ]
        specs.append(whole(right.shape))
    operands += others
    specs += [
        pl.BlockSpec((blk, other.shape[1]), lambda i, par: (every * i + par[0], 0))
        for other in others
    ]
    total = sum(mat.shape[1] for _, mat in products) + sum(other.shape[1] for other in others)
    counts = [len(left) for left, _ in products]
    out_spec = pl.BlockSpec((blk, total), lambda i, par: (i, 0))
    if added is not None:
        operands.append(added)
        specs.append(out_spec)

    def kernel(par_ref, *refs):
        o_ref, refs = refs[-1], list(refs[:-1])
        a_ref = refs.pop() if added is not None else None

        def give(value, place):
            columns = slice(place, place + value.shape[1])
            if a_ref is not None:
                value = value.astype(f32) + a_ref[:, columns].astype(f32)
            o_ref[:, columns] = value.astype(bf16)
            return columns.stop

        place = 0
        for count in counts:
            rows = jnp.concatenate([ref[...] for ref in refs[:count]], axis=0)
            place = give(across(rows, refs[count][...]), place)
            refs = refs[count + 1 :]
        for ref in refs:
            place = give(ref[...], place)

    return pl.pallas_call(
        kernel,
        out_shape=jax.ShapeDtypeStruct((width // every, total), bf16),
        grid_spec=pltpu.PrefetchScalarGridSpec(
            num_scalar_prefetch=1,
            grid=(width // blk // every,),
            in_specs=specs,
            out_specs=out_spec,
        ),
        compiler_params=pltpu.CompilerParams(vmem_limit_bytes=60 * MIB),
        cost_estimate=small_cost(1024),
        name=name,
    )(parity.reshape(1), *operands)


def crossed(piece, axis, bit):
    length = lax.axis_size(axis)
    return lax.ppermute(piece, axis, [(i, i ^ bit) for i in range(length)])


def spread_start(piece, axis):
    held = {0: piece}
    bit = lax.axis_size(axis) // 2
    while bit:
        held.update({k | bit: crossed(held[k], axis, bit) for k in list(held)})
        bit //= 2
    return [held[k] for k in range(1, len(held))]


def fold_start(chunks, axis):
    terms = {k: [chunk] for k, chunk in enumerate(chunks)}
    bit = 1
    while bit < len(chunks):
        for k in [k for k in terms if k & bit]:
            going = terms.pop(k)
            going = going[0] if len(going) == 1 else summed(going).astype(bf16)
            terms[k ^ bit].append(crossed(going, axis, bit))
        bit *= 2
    return terms[0]


def folded(chunks, axis):
    return summed(fold_start(chunks, axis))


def with_work(arrived, work):
    return lax.optimization_barrier((arrived, work))


def passed_along(shard, axis, by):
    length = lax.axis_size(axis)
    pairs = [(i, i + by) for i in range(length) if 0 <= i + by < length]
    return lax.ppermute(shard, axis, pairs)


def summed(terms):
    total = terms[0].astype(f32)
    for term in terms[1:]:
        total = total + term.astype(f32)
    return total


def rank_among(keys_own):
    count = keys_own.shape[0]
    place = jnp.arange(count, dtype=jnp.int32)
    same = (keys_own[None, :] == keys_own[:, None]) & (place[None, :] < place[:, None])
    return jnp.sum(same.astype(jnp.int32), axis=1)


def plan(lengths, order, micro, block_rows):
    devices = lax.axis_size("dp")
    parts = lax.axis_size("tensor")
    me = lax.axis_index("dp")
    part = lax.axis_index("tensor")
    tok = micro * block_rows
    own = tok // parts
    stretch = devices * block_rows
    seqs = lengths.shape[0]
    given_len = jnp.take(lengths, order)
    given_start = jnp.cumsum(given_len) - given_len
    dealt_start = jnp.cumsum(lengths) - lengths
    seq_ids = jnp.arange(seqs, dtype=jnp.int32)
    shift_given = jnp.take(dealt_start, order) - given_start
    pieces = tok // LMIN + 2
    runs = tok // stretch + 1
    per_piece = block_rows * (-(-tok // stretch)) + (parts - 1) * runs
    capacity = -(-(pieces * (per_piece // parts) + 1) // 8) * 8
    kept = -(-(tok // parts + seqs + 1) // 8) * 8

    def pick(table, index):
        return jnp.sum(jnp.where(index[:, None] == seq_ids[None, :], table[None, :], 0), axis=1)

    local = jnp.arange(tok, dtype=jnp.int32)
    stream = local // block_rows * stretch + me * block_rows + local % block_rows
    arrival = jnp.sum((stream[:, None] >= given_start[None, 1:]).astype(jnp.int32), axis=1)
    dealt = stream + pick(shift_given, arrival)
    target = dealt // tok
    quarter = dealt % parts
    send_slot = target * capacity + rank_among(target * parts + quarter)
    send_slot = jnp.where(quarter == part, send_slot, -1)
    keep_rank = rank_among(quarter)
    keep_slot = (part ^ quarter) * kept + keep_rank

    place = me * tok + jnp.arange(own, dtype=jnp.int32) * parts + part
    own_seq = jnp.sum((place[:, None] >= dealt_start[None, 1:]).astype(jnp.int32), axis=1)
    shift_dealt = jnp.sum(
        jnp.where(order[None, :] == seq_ids[:, None], -shift_given[None, :], 0), axis=1
    )
    anchor = place + pick(shift_dealt, own_seq)
    source = anchor % stretch // block_rows
    prior = (anchor[None, :] < anchor[:, None]) & (source[None, :] == source[:, None])
    recv_slot = source * capacity + jnp.sum(prior.astype(jnp.int32), axis=1)

    total = devices * capacity
    slots = jnp.arange(total, dtype=jnp.int32)
    sender = (slots[:, None] == send_slot[None, :]).astype(bf16)
    receiver = (recv_slot[:, None] == slots[None, :]).astype(bf16)
    mine = jnp.where(quarter == part, keep_rank, -1)
    chosen = (jnp.arange(kept, dtype=jnp.int32)[:, None] == mine[None, :]).astype(bf16)
    compact = against(chosen, sender, bf16)
    homing = (
        keep_slot[:, None] == jnp.arange(parts * kept, dtype=jnp.int32)[None, :]
    ).astype(bf16)

    held = part ^ jnp.arange(parts, dtype=jnp.int32)
    rows = (jnp.arange(own, dtype=jnp.int32)[None, :] * parts + held[:, None]).reshape(tok)
    both = me * tok + jnp.concatenate([rows - tok, rows])
    ext_seq = jnp.sum((both[:, None] >= dealt_start[None, 1:]).astype(jnp.int32), axis=1)
    start = pick(dealt_start, ext_seq[tok:])
    high_bound = both[tok:]
    low_bound = jnp.maximum(start, high_bound - (WIN - 1))
    return sender, receiver, compact, homing, (low_bound, high_bound, both), high_bound - start


def body(
    hidden_in,
    layer_inputs,
    out_grad,
    lengths,
    order,
    w_query,
    w_keyval,
    w_out,
    w_left,
    w_right,
    w_gateup,
    w_down,
    w_pergate,
    w_perproj,
    gains,
    head_gains,
):
    devices = lax.axis_size("dp")
    me = lax.axis_index("dp")
    parts = lax.axis_size("tensor")
    part = lax.axis_index("tensor")
    micro, block_rows, width = hidden_in.shape
    per_width = layer_inputs.shape[2]
    tok = micro * block_rows
    assert tok == WIN
    sender, receiver, compact, homing, bounds, own_pos = plan(lengths, order, micro, block_rows)

    kv_cols = part // (parts // KVH) * HD
    kv_own = lax.dynamic_slice_in_dim(w_keyval, kv_cols, HD, 2)
    gains_high = lax.reduce_precision(gains, 8, 7)
    gains_low = (gains - gains_high).astype(bf16)
    gain_cols = jnp.concatenate([gains_high.astype(bf16), gains_low], axis=0)
    gain_cols = jnp.pad(gain_cols, ((0, LANES - gain_cols.shape[0]), (0, 0))).T
    q_width = w_query.shape[1]
    rank = w_left.shape[1]

    def gather_columns(pieces):
        marks = [0]
        for piece in pieces:
            marks.append(marks[-1] + piece.shape[1])
        full = lax.all_gather(jnp.concatenate(pieces, axis=1), "dp", axis=0, tiled=True)
        return full, [full[:, a:b] for a, b in zip(marks[:-1], marks[1:])]

    first = [w_query, kv_own[0], kv_own[1], w_out.T, w_left, w_right.T, gain_cols]
    bundle_a, (wq, wk, wv, wo_t, wl, wr_t, gain_f) = gather_columns(first)
    units = w_down.shape[0]
    packed_in = product(sender, hidden_in.reshape(tok, width), bf16)
    come_in = lax.all_to_all(packed_in, "dp", 0, 0, tiled=True)
    low_inputs = product(receiver, come_in, bf16)
    inputs = low_inputs.astype(f32)
    token_pieces = spread_start(low_inputs, "tensor")
    w_ff, _ = gather_columns([w_gateup[0], w_gateup[1], w_down.T])
    w_gains = gain_f.T
    gains_f = w_gains[:6].astype(f32) + w_gains[6:12].astype(f32)
    angles = own_pos.astype(f32)[:, None] * frequencies()

    def homeward(rows_own):
        return lax.all_to_all(across(receiver, rows_own, bf16), "dp", 0, 0, tiled=True)

    block = width // devices
    paired = devices > 1 and block % (2 * LANES) == 0
    low_bit = me % 2
    groups = [list(range(k, devices, 2)) for k in range(2)] if paired else None

    def scattered(grads):
        return lax.psum_scatter(
            grads, "dp", scatter_dimension=0, axis_index_groups=groups, tiled=True
        )

    def grads_leaving(make):
        return make(block, 2, 1 - low_bit) if paired else make(2 * LANES, 1, me * 0)

    def beside_first(chunks, work):
        chunks = list(chunks)
        chunks[-2], work = with_work(chunks[-2], work)
        return chunks, work

    def grads_come(leaving):
        return crossed(leaving, "dp", 1) if paired else leaving

    def grads_staying(make, come):
        return make(block, 2, low_bit, come) if paired else come

    cosine, sine = jnp.cos(angles), jnp.sin(angles)
    heads = q_width // HD
    all_in, raw, queries, own_kv = project(
        [low_inputs] + token_pieces, gains_f[:1], bundle_a, head_gains, cosine, sine, heads
    )
    normal_in = normed(inputs, gains_f[0])
    low_in = normal_in.astype(bf16)
    tails = passed_along(own_kv, "dp", 1)
    low_att, branch_parts = attend(queries, tails, own_kv, *bounds, bundle_a, parts)
    branch = folded(branch_parts, "tensor")

    low_rank = product(low_in, wl, bf16)
    laurel_raw = against(low_rank, wr_t)
    first_sum = (
        inputs + normed(branch, gains_f[1]) + normal_in + normed(laurel_raw, gains_f[2])
    ) * half_root
    low_mid = normed(first_sum, gains_f[3]).astype(bf16)

    all_mid = [low_mid] + spread_start(low_mid, "tensor")
    rest_in = jnp.concatenate(
        [layer_inputs.reshape(tok, per_width), out_grad.reshape(tok, width)], axis=1
    )
    third = [w_pergate, w_perproj.T]
    rest_out = product(sender, rest_in, bf16)
    (rest_out, third), w_ff = with_work((rest_out, third), w_ff)
    _, (wg, wp_t) = gather_columns(third)
    come_rest = lax.all_to_all(rest_out, "dp", 0, 0, tiled=True)
    gate_raw, upward, low_hidden, feed_parts = feed_forward(all_mid, w_ff, units)
    feed_parts, come_rest = with_work(feed_parts, come_rest)
    fed_pieces = fold_start(feed_parts, "tensor")
    rest = product(receiver, come_rest, bf16)
    layer_in = rest[:, :per_width].astype(f32)
    cotangent = rest[:, per_width:].astype(f32)
    feed_raw = summed(fed_pieces)

    second_sum = first_sum + normed(feed_raw, gains_f[4])
    low_second = second_sum.astype(bf16)
    pre_gate = product(low_second, wg)
    low_gated = (gelu_tanh(pre_gate) * layer_in).astype(bf16)
    per_raw = against(low_gated, wp_t)
    result = second_sum + normed(per_raw, gains_f[5])

    _, back_per = jax.vjp(normed, per_raw, gains_f[5])
    per_grad, grad_g5 = back_per(cotangent)
    low_per = per_grad.astype(bf16)
    gated_grad = product(low_per, wp_t)
    gelu_out, back_gelu = jax.vjp(gelu_tanh, pre_gate)
    low_pre = back_gelu(gated_grad * layer_in)[0].astype(bf16)
    layer_grad = gated_grad * gelu_out
    second_grad = cotangent + against(low_pre, wg)
    _, back_feed = jax.vjp(normed, feed_raw, gains_f[4])
    feed_grad, grad_g4 = back_feed(second_grad)
    low_feed = feed_grad.astype(bf16)

    feed_pieces = spread_start(low_feed, "tensor")
    grad_perproj = across(low_per, low_gated, bf16)
    grad_pergate = across(low_second, low_pre, bf16)
    low_result = jnp.concatenate([result.astype(bf16), layer_grad.astype(bf16)], axis=1)
    come_one = homeward(low_result)
    feed_pieces, (grad_perproj, grad_pergate, come_one) = with_work(
        feed_pieces, (grad_perproj, grad_pergate, come_one)
    )
    all_feed = [low_feed] + feed_pieces

    home_one = product(compact, come_one, bf16)
    home_pieces = spread_start(home_one, "tensor")
    low_gate, low_up, mid_parts = feed_back(all_feed, w_ff, gate_raw, upward)
    mid_parts, home_pieces[0] = with_work(mid_parts, home_pieces[0])
    mid_parts, home_pieces[1] = with_work(mid_parts, home_pieces[1])

    def ff_grads_of(*where):
        return column_grads(
            [(all_mid, low_gate), (all_mid, low_up), (all_feed, low_hidden)],
            [grad_pergate, grad_perproj],
            "feed_grads",
            *where,
        )

    mid_parts, ff_leaving = beside_first(mid_parts, grads_leaving(ff_grads_of))
    mid_pieces = fold_start(mid_parts, "tensor")
    ff_grads = grads_staying(ff_grads_of, grads_come(ff_leaving))
    mid_pieces, ff_grads = with_work(mid_pieces, ff_grads)
    s_ff = scattered(ff_grads)
    mid_grad = summed(mid_pieces)

    _, back_mid = jax.vjp(normed, first_sum, gains_f[3])
    first_part, grad_g3 = back_mid(mid_grad)
    shared = (second_grad + first_part) * half_root
    _, back_laurel = jax.vjp(normed, laurel_raw, gains_f[2])
    laurel_grad, grad_g2 = back_laurel(shared)
    low_laurel = laurel_grad.astype(bf16)
    _, back_branch = jax.vjp(normed, branch, gains_f[1])
    branch_grad, grad_g1 = back_branch(shared)
    low_branch = branch_grad.astype(bf16)

    branch_pieces = spread_start(low_branch, "tensor")
    low_rank_grad = product(low_laurel, wr_t, bf16)
    grad_right = across(low_laurel, low_rank, bf16)
    grad_left = across(low_in, low_rank_grad, bf16)
    small = jnp.concatenate([grad_left, grad_right], axis=1)
    gain_part = jnp.stack([grad_g1, grad_g2, grad_g3, grad_g4, grad_g5])
    branch_pieces, (small, gain_part) = with_work(branch_pieces, (small, gain_part))
    all_branch = [low_branch] + branch_pieces

    query_grad, own_grad, halo_grad = attend_back(
        queries, tails, own_kv, all_branch, *bounds, bundle_a
    )
    query_grad, home_pieces[-1] = with_work(query_grad, home_pieces[-1])
    next_grad = passed_along(halo_grad, "dp", -1)
    low_qkv, head_grads, in_parts = project_back(
        query_grad, own_grad, next_grad, raw, head_gains, cosine, sine, bundle_a, parts
    )

    head_cols = head_grads.reshape(-1, width // devices)
    head_count = head_cols.shape[0]
    head_cols = jnp.tile(head_cols, (1, devices))
    last_cols = jnp.concatenate([gain_part, head_cols], axis=0).astype(bf16)
    last_cols = jnp.pad(last_cols, ((0, LANES - last_cols.shape[0]), (0, 0))).T
    def at_grads_of(*where):
        return column_grads(
            [([all_in], low_qkv), (all_branch, low_att)],
            [small, last_cols],
            "attention_grads",
            *where,
        )

    in_parts, at_leaving = beside_first(in_parts, grads_leaving(at_grads_of))
    in_pieces = fold_start(in_parts, "tensor")
    in_pieces, at_come = with_work(in_pieces, grads_come(at_leaving))
    in_attn = summed(in_pieces)
    normal_grad = in_attn + against(low_rank_grad, wl) + shared
    _, back_in = jax.vjp(normed, inputs, gains_f[0])
    in_part, grad_g0 = back_in(normal_grad)
    input_grad = shared + in_part
    extra = jnp.pad(
        grad_g0.reshape(devices, 1, block),
        ((0, 0), (receiver.shape[1] // devices - 1, 0), (0, width - block)),
    )
    sent_two = across(receiver, input_grad.astype(bf16)) + extra.reshape(-1, width)
    come_two = lax.all_to_all(sent_two.astype(bf16), "dp", 0, 0, tiled=True)
    at_grads = grads_staying(at_grads_of, at_come)
    at_grads, s_ff = with_work(at_grads, s_ff)
    s_at = scattered(at_grads)
    early = s_ff[:, 3 * units :]
    bit = 1
    while bit < parts:
        early = summed([early, crossed(early, "tensor", bit)])
        early = early.astype(bf16) if 2 * bit < parts else early
        bit *= 2
    come_two, early = with_work(come_two, early)
    g0_part = jnp.sum(come_two.reshape(devices, -1, width)[:, -1, :block].astype(f32), axis=0)
    home_two = product(compact, come_two) + jnp.pad(
        g0_part[None], ((compact.shape[0] - 1, 0), (0, width - block))
    )
    o_kv = q_width + 2 * HD
    o_small = o_kv + w_out.shape[0]
    kv_cols = 2 * HD
    exchanged = jnp.concatenate([s_at[:, q_width:o_kv], s_at[:, o_small:]], axis=1)
    bit = 1
    while bit < parts // KVH:
        exchanged = summed([exchanged, crossed(exchanged, "tensor", bit)]).astype(bf16)
        bit *= 2
    home_two = home_two.astype(bf16)
    two_pieces, exchanged = with_work(spread_start(home_two, "tensor"), exchanged)
    all_two = jnp.concatenate([home_two] + two_pieces, axis=0)
    back_two = product(homing, all_two, bf16)
    g0_terms = all_two.reshape(parts, -1, width)[:, -1, :block].astype(f32)
    while g0_terms.shape[0] > 1:
        middle = g0_terms.shape[0] // 2
        g0_terms = g0_terms[:middle] + g0_terms[middle:]

    shard_gateup = jnp.stack([s_ff[:, :units], s_ff[:, units : 2 * units]]).astype(f32)
    shard_down = s_ff[:, 2 * units : 3 * units].T.astype(f32)
    shard_query = s_at[:, :q_width].astype(f32)
    shard_out = s_at[:, o_kv:o_small].T.astype(f32)
    arrived = crossed(exchanged, "tensor", bit)
    kv_sum, kv_other = exchanged[:, :kv_cols], arrived[:, :kv_cols]
    small_sum = summed([exchanged[:, kv_cols:], arrived[:, kv_cols:]])
    shard_left = small_sum[:, :rank]
    shard_right = small_sum[:, rank : 2 * rank].T
    shard_pergate = early[:, :per_width]
    shard_perproj = early[:, per_width:].T
    last_sum = small_sum[:, 2 * rank :].T
    shard_gains = jnp.concatenate([g0_terms, last_sum[:5]], axis=0)
    head_total = last_sum[5 : 5 + head_count].reshape(2, HD)
    upper = part // (parts // KVH) == 1
    low_head = jnp.where(upper, kv_other, kv_sum).astype(f32)
    high_head = jnp.where(upper, kv_sum, kv_other).astype(f32)
    shard_keyval = jnp.stack(
        [
            jnp.concatenate([low_head[:, :HD], high_head[:, :HD]], axis=1),
            jnp.concatenate([low_head[:, HD:], high_head[:, HD:]], axis=1),
        ]
    )
    back_one = product(homing, jnp.concatenate([home_one] + home_pieces, axis=0), bf16)
    return (
        back_one[:, :width].reshape(micro, block_rows, width),
        back_two.reshape(micro, block_rows, width),
        back_one[:, width:].reshape(micro, block_rows, per_width),
        shard_query,
        shard_keyval,
        shard_out,
        shard_left,
        shard_right,
        shard_gateup,
        shard_down,
        shard_pergate,
        shard_perproj,
        shard_gains,
        head_total,
    )


def solution(mesh):
    placed = (
        P(None, "dp", None),
        P(None, "dp", None),
        P(None, "dp", None),
        P(),
        P(),
        P("dp", "tensor"),
        P(None, "dp", None),
        P("tensor", "dp"),
        P("dp", None),
        P(None, "dp"),
        P(None, "dp", "tensor"),
        P("tensor", "dp"),
        P("dp", None),
        P(None, "dp"),
        P(None, "dp"),
        P(),
    )
    return jax.shard_map(
        body,
        mesh=mesh,
        in_specs=placed,
        out_specs=(
            P(None, "dp", None),
            P(None, "dp", None),
            P(None, "dp", None),
            P("dp", "tensor"),
            P(None, "dp", None),
            P("tensor", "dp"),
            P("dp", None),
            P(None, "dp"),
            P(None, "dp", "tensor"),
            P("tensor", "dp"),
            P("dp", None),
            P(None, "dp"),
            P(None, "dp"),
            P(),
        ),
        check_vma=False,
    )
```

```python
import jax
import jax.numpy as jnp
from jax import lax
from jax.experimental import pallas as pl
from jax.experimental.pallas import tpu as pltpu
from jax.sharding import PartitionSpec as P

KVH = 2
HD = 256
WIN = 512
LMIN = 1024
LANES = 128

half_root = 0.7071067811865476
masked_value = -1e30
bf16 = jnp.bfloat16
f32 = jnp.float32


def normed(values_in, gain_vec):
    norm_scale = lax.rsqrt(jnp.mean(values_in * values_in, axis=-1, keepdims=True) + 1e-06)
    return values_in * norm_scale * gain_vec


def rotate(values_in, angles):
    half_dim = values_in.shape[-1] // 2
    first_half = values_in[..., :half_dim]
    second_half = values_in[..., half_dim:]
    cosine = jnp.cos(angles)
    sine_part = jnp.sin(angles)
    return jnp.concatenate(
        [
            first_half * cosine - second_half * sine_part,
            second_half * cosine + first_half * sine_part,
        ],
        axis=-1,
    )


def gelu_tanh(values_in):
    return jax.nn.gelu(values_in, approximate=True)


def glu_pair(gate_raw, upward):
    return gelu_tanh(gate_raw) * upward


def value_map(raw_value):
    return normed(raw_value, 1.0)


def product(left_mat, right_mat, kind=f32):
    return jnp.dot(left_mat, right_mat, preferred_element_type=f32).astype(kind)


def against(left_mat, right_mat, kind=f32):
    return lax.dot_general(
        left_mat, right_mat, (((1,), (1,)), ((), ())), preferred_element_type=f32
    ).astype(kind)


def across(left_mat, right_mat, kind=f32):
    return lax.dot_general(
        left_mat, right_mat, (((0,), (0,)), ((), ())), preferred_element_type=f32
    ).astype(kind)


def frequencies():
    half_dim = HD // 2
    return jnp.power(10000.0, -2.0 * jnp.arange(half_dim, dtype=f32) / HD)


MIB = 1 << 20


def small_cost(flops):
    return pl.CostEstimate(flops=flops, bytes_accessed=1024, transcendentals=0)


def whole(shape):
    zeros = (0,) * len(shape)
    return pl.BlockSpec(shape, lambda *_: zeros, pipeline_mode=pl.Buffered(1))


def in_pieces_of(count, rows, width):
    return [whole((rows, width)) for _ in range(count)]


def gather_rows(piece_refs, full_ref):
    rows = piece_refs[0].shape[0]
    for index, piece in enumerate(piece_refs):
        full_ref[index * rows : (index + 1) * rows, :] = piece[...]


def give_rows(step, value, piece_refs):
    rows = piece_refs[0].shape[0]
    each = value.shape[0] // rows
    for index, piece in enumerate(piece_refs):
        place = index % each * rows

        @pl.when(step == index // each)
        def _():
            piece[...] = value[place : place + rows, :].astype(bf16)


def mean_scale(values):
    return lax.rsqrt(jnp.mean(values * values, axis=1, keepdims=True) + 1e-06)


def turned(values, cosine, sine):
    half = values.shape[1] // 2
    first, second = values[:, :half], values[:, half:]
    return jnp.concatenate(
        [first * cosine - second * sine, second * cosine + first * sine], axis=1
    )


def project(pieces, gain, bundle, head_gains, cosine, sine, heads):
    count = len(pieces)
    own, width = pieces[0].shape
    tok = count * own
    total = (heads + 2) * HD
    rows = tok // 2

    def kernel(*refs):
        piece_refs = refs[:count]
        g_ref, w_ref, hg_ref, c_ref, s_ref, in_ref, raw_ref, q_ref, kv_ref, full = refs[count:]
        step = pl.program_id(0)

        @pl.when(step == 0)
        def _():
            gather_rows(piece_refs, full)

        x = full[pl.ds(pl.multiple_of(step * rows, rows), rows), :].astype(f32)
        low = (x * mean_scale(x) * g_ref[...]).astype(bf16)
        in_ref[...] = low
        raw = product(low, w_ref[...])
        raw_ref[...] = raw
        cosine, sine = c_ref[...], s_ref[...]
        for head in range(heads):
            part = raw[:, head * HD : (head + 1) * HD]
            part = part * mean_scale(part) * hg_ref[0:1, :]
            q_ref[:, head * HD : (head + 1) * HD] = turned(part, cosine, sine).astype(bf16)
        part = raw[:, heads * HD : (heads + 1) * HD]
        part = part * mean_scale(part) * hg_ref[1:2, :]
        kv_ref[:, :HD] = turned(part, cosine, sine).astype(bf16)
        part = raw[:, (heads + 1) * HD :]
        kv_ref[:, HD:] = (part * mean_scale(part)).astype(bf16)

    def row_block(columns):
        return pl.BlockSpec((rows, columns), lambda i: (i, 0))

    return pl.pallas_call(
        kernel,
        out_shape=(
            jax.ShapeDtypeStruct((tok, width), bf16),
            jax.ShapeDtypeStruct((tok, total), f32),
            jax.ShapeDtypeStruct((tok, heads * HD), bf16),
            jax.ShapeDtypeStruct((tok, 2 * HD), bf16),
        ),
        grid=(2,),
        in_specs=in_pieces_of(count, own, width)
        + [
            whole((1, width)),
            whole((width, total)),
            whole((2, HD)),
            row_block(HD // 2),
            row_block(HD // 2),
        ],
        out_specs=(row_block(width), row_block(total), row_block(heads * HD), row_block(2 * HD)),
        scratch_shapes=[pltpu.VMEM((tok, width), bf16)],
        compiler_params=pltpu.CompilerParams(vmem_limit_bytes=60 * MIB),
        cost_estimate=small_cost(2 * tok * width * total),
        name="project",
    )(*pieces, gain, bundle, head_gains, cosine, sine)


def attend(queries, tails, own_kv, low_bound, high_bound, key_place, bundle, count):
    tok, total = queries.shape
    heads = total // HD
    width = bundle.shape[0]
    span = 2 * tok
    rows = tok // 2
    first = heads + 2

    def kernel(q_ref, t_ref, o_ref, lo_ref, hi_ref, kp_ref, w_ref, att_ref, *rest):
        piece_refs, (kv, acc) = rest[:count], rest[count:]
        step, head = pl.program_id(0), pl.program_id(1)

        @pl.when((step == 0) & (head == 0))
        def _():
            kv[:tok, :] = t_ref[...]
            kv[tok:, :] = o_ref[...]

        scores = against(q_ref[...], kv[:, :HD])
        kp = kp_ref[...]
        allowed = (kp >= lo_ref[...]) & (kp <= hi_ref[...])
        masked = jnp.where(allowed, scores, masked_value)
        raised = jnp.exp(masked - jnp.max(masked, axis=1, keepdims=True))
        inverse = 1.0 / jnp.sum(raised, axis=1, keepdims=True)
        attended = product((raised * inverse).astype(bf16), kv[:, HD:], bf16)
        att_ref[...] = attended
        part = against(attended, w_ref[...])

        @pl.when(head == 0)
        def _():
            acc[...] = part

        @pl.when(head > 0)
        def _():
            acc[...] += part

        @pl.when(head == heads - 1)
        def _():
            give_rows(step, acc[...], piece_refs)

    result = pl.pallas_call(
        kernel,
        out_shape=[jax.ShapeDtypeStruct((tok, total), bf16)]
        + [jax.ShapeDtypeStruct((tok // count, width), bf16)] * count,
        grid=(2, heads),
        in_specs=[
            pl.BlockSpec((rows, HD), lambda i, h: (i, h)),
            whole((tok, 2 * HD)),
            whole((tok, 2 * HD)),
            pl.BlockSpec((rows, 1), lambda i, h: (i, 0)),
            pl.BlockSpec((rows, 1), lambda i, h: (i, 0)),
            whole((1, span)),
            pl.BlockSpec((width, HD), lambda i, h: (0, first + h)),
        ],
        out_specs=[pl.BlockSpec((rows, HD), lambda i, h: (i, h))]
        + [pl.BlockSpec((tok // count, width), lambda i, h: (0, 0))] * count,
        scratch_shapes=[pltpu.VMEM((span, 2 * HD), bf16), pltpu.VMEM((rows, width), f32)],
        compiler_params=pltpu.CompilerParams(vmem_limit_bytes=60 * MIB),
        cost_estimate=small_cost(4 * tok * span * total),
        name="attend",
    )(
        queries,
        tails,
        own_kv,
        low_bound[:, None],
        high_bound[:, None],
        key_place[None, :],
        bundle,
    )
    return result[0], result[1:]


def attend_back(queries, tails, own_kv, pieces, low_bound, high_bound, key_place, bundle):
    tok, total = queries.shape
    heads = total // HD
    count = len(pieces)
    own, width = pieces[0].shape
    span = 2 * tok
    rows = tok // 2
    first = heads + 2

    def kernel(q_ref, t_ref, o_ref, lo_ref, hi_ref, kp_ref, w_ref, *rest):
        piece_refs = rest[:count]
        dq_ref, own_ref, halo_ref, kv, full, acc = rest[count:]
        head, step = pl.program_id(0), pl.program_id(1)
        begin = (head == 0) & (step == 0)

        @pl.when(begin)
        def _():
            kv[:tok, :] = t_ref[...]
            kv[tok:, :] = o_ref[...]
            gather_rows(piece_refs, full)

        here = pl.ds(pl.multiple_of(step * rows, rows), rows)
        g = product(full[here, :], w_ref[...], bf16)
        q, k, v = q_ref[...], kv[:, :HD], kv[:, HD:]
        scores = against(k, q)
        kp = kp_ref[...]
        allowed = (kp >= lo_ref[...]) & (kp <= hi_ref[...])
        masked = jnp.where(allowed, scores, masked_value)
        raised = jnp.exp(masked - jnp.max(masked, axis=0, keepdims=True))
        probs = raised * (1.0 / jnp.sum(raised, axis=0, keepdims=True))
        prob_grad = against(v, g)
        centre = jnp.sum(probs * prob_grad, axis=0, keepdims=True)
        score_grad = (probs * (prob_grad - centre)).astype(bf16)
        dq_ref[...] = across(score_grad, k)
        dk_part = product(score_grad, q)
        dv_part = product(probs.astype(bf16), g)

        @pl.when(begin)
        def _():
            acc[:, :HD] = dk_part
            acc[:, HD:] = dv_part

        @pl.when(jnp.logical_not(begin))
        def _():
            acc[:, :HD] += dk_part
            acc[:, HD:] += dv_part

        @pl.when((head == heads - 1) & (step == 1))
        def _():
            halo_ref[...] = acc[:tok, :].astype(bf16)
            own_ref[...] = acc[tok:, :]

    return pl.pallas_call(
        kernel,
        out_shape=(
            jax.ShapeDtypeStruct((tok, total), f32),
            jax.ShapeDtypeStruct((tok, 2 * HD), f32),
            jax.ShapeDtypeStruct((tok, 2 * HD), bf16),
        ),
        grid=(heads, 2),
        in_specs=[
            pl.BlockSpec((rows, HD), lambda h, i: (i, h)),
            whole((tok, 2 * HD)),
            whole((tok, 2 * HD)),
            pl.BlockSpec((1, rows), lambda h, i: (0, i)),
            pl.BlockSpec((1, rows), lambda h, i: (0, i)),
            whole((span, 1)),
            pl.BlockSpec((width, HD), lambda h, i: (0, first + h)),
        ]
        + in_pieces_of(count, own, width),
        out_specs=(
            pl.BlockSpec((rows, HD), lambda h, i: (i, h)),
            pl.BlockSpec((tok, 2 * HD), lambda h, i: (0, 0)),
            pl.BlockSpec((tok, 2 * HD), lambda h, i: (0, 0)),
        ),
        scratch_shapes=[
            pltpu.VMEM((span, 2 * HD), bf16),
            pltpu.VMEM((tok, width), bf16),
            pltpu.VMEM((span, 2 * HD), f32),
        ],
        compiler_params=pltpu.CompilerParams(vmem_limit_bytes=60 * MIB),
        cost_estimate=small_cost(10 * tok * span * total),
        name="attend_back",
    )(
        queries,
        tails,
        own_kv,
        low_bound[None, :],
        high_bound[None, :],
        key_place[:, None],
        bundle,
        *pieces,
    )


def project_back(query_grad, own_grad, next_grad, raw, head_gains, cosine, sine, bundle, count):
    tok, total = raw.shape
    heads = query_grad.shape[1] // HD
    width = bundle.shape[0]
    rows = tok // 2

    def kernel(dq_ref, o_ref, n_ref, raw_ref, hg_ref, c_ref, s_ref, w_ref, low_ref, hg_out, *pieces):
        step = pl.program_id(0)
        cosine, sine = c_ref[...], s_ref[...]
        both = o_ref[...] + n_ref[...].astype(f32)
        raw_rows = raw_ref[...]

        def norm_back(grad, values, gain):
            scale = mean_scale(values)
            weighted = grad if gain is None else grad * gain
            centre = jnp.mean(weighted * values, axis=1, keepdims=True)
            back = scale * weighted - values * (scale * scale * scale * centre)
            return back, jnp.sum(grad * values * scale, axis=0, keepdims=True)

        gain_grad = jnp.zeros((1, HD), f32)
        for head in range(heads):
            columns = slice(head * HD, (head + 1) * HD)
            grad = turned(dq_ref[:, columns], cosine, -sine)
            back, part = norm_back(grad, raw_rows[:, columns], hg_ref[0:1, :])
            low_ref[:, columns] = back.astype(bf16)
            gain_grad = gain_grad + part
        columns = slice(heads * HD, (heads + 1) * HD)
        grad = turned(both[:, :HD], cosine, -sine)
        back, key_gain = norm_back(grad, raw_rows[:, columns], hg_ref[1:2, :])
        low_ref[:, columns] = back.astype(bf16)
        columns = slice((heads + 1) * HD, (heads + 2) * HD)
        back, _ = norm_back(both[:, HD:], raw_rows[:, columns], None)
        low_ref[:, columns] = back.astype(bf16)

        @pl.when(step == 0)
        def _():
            hg_out[0:1, :] = gain_grad
            hg_out[1:2, :] = key_gain

        @pl.when(step > 0)
        def _():
            hg_out[0:1, :] += gain_grad
            hg_out[1:2, :] += key_gain

        give_rows(step, against(low_ref[...], w_ref[...]), pieces)

    def row_block(columns):
        return pl.BlockSpec((rows, columns), lambda i: (i, 0))

    result = pl.pallas_call(
        kernel,
        out_shape=[
            jax.ShapeDtypeStruct((tok, total), bf16),
            jax.ShapeDtypeStruct((2, HD), f32),
        ]
        + [jax.ShapeDtypeStruct((tok // count, width), bf16)] * count,
        grid=(2,),
        in_specs=[
            row_block(heads * HD),
            row_block(2 * HD),
            row_block(2 * HD),
            row_block(total),
            whole((2, HD)),
            row_block(HD // 2),
            row_block(HD // 2),
            whole((width, total)),
        ],
        out_specs=[row_block(total), pl.BlockSpec((2, HD), lambda i: (0, 0))]
        + [pl.BlockSpec((tok // count, width), lambda i: (0, 0))] * count,
        compiler_params=pltpu.CompilerParams(vmem_limit_bytes=60 * MIB),
        cost_estimate=small_cost(2 * tok * width * total),
        name="project_back",
    )(query_grad, own_grad, next_grad, raw, head_gains, cosine, sine, bundle)
    return result[0], result[1], result[2:]


def feed_forward(pieces, w_ff, units):
    count = len(pieces)
    own, width = pieces[0].shape
    tok = count * own
    blk = 512

    def kernel(*refs):
        piece_refs = refs[:count]
        g_ref, u_ref, d_ref, gate_ref, up_ref, hid_ref = refs[count : count + 6]
        out_refs, (full, acc) = refs[count + 6 : 2 * count + 6], refs[2 * count + 6 :]
        step = pl.program_id(0)

        @pl.when(step == 0)
        def _():
            gather_rows(piece_refs, full)

        mid_rows = full[...]
        gate = product(mid_rows, g_ref[...])
        up = product(mid_rows, u_ref[...])
        hidden = glu_pair(gate, up).astype(bf16)
        gate_ref[...] = gate.astype(bf16)
        up_ref[...] = up.astype(bf16)
        hid_ref[...] = hidden
        part = against(hidden, d_ref[...])

        @pl.when(step == 0)
        def _():
            acc[...] = part

        @pl.when(step > 0)
        def _():
            acc[...] += part

        @pl.when(step == pl.num_programs(0) - 1)
        def _():
            for index, piece in enumerate(out_refs):
                piece[...] = acc[index * own : (index + 1) * own, :].astype(bf16)

    plane = lambda k: pl.BlockSpec((width, blk), lambda j: (0, k * (units // blk) + j))
    columns = pl.BlockSpec((tok, blk), lambda j: (0, j))
    result = pl.pallas_call(
        kernel,
        out_shape=[jax.ShapeDtypeStruct((tok, units), bf16)] * 3
        + [jax.ShapeDtypeStruct((own, width), bf16)] * count,
        grid=(units // blk,),
        in_specs=in_pieces_of(count, own, width) + [plane(0), plane(1), plane(2)],
        out_specs=[columns] * 3 + [pl.BlockSpec((own, width), lambda j: (0, 0))] * count,
        scratch_shapes=[pltpu.VMEM((tok, width), bf16), pltpu.VMEM((tok, width), f32)],
        compiler_params=pltpu.CompilerParams(vmem_limit_bytes=60 * MIB),
        cost_estimate=small_cost(6 * tok * width * units),
        name="feed_forward",
    )(*pieces, w_ff, w_ff, w_ff)
    return result[0], result[1], result[2], result[3:]


def feed_back(pieces, w_ff, gate_raw, upward):
    count = len(pieces)
    own, width = pieces[0].shape
    tok = count * own
    units = upward.shape[1]
    blk = 512

    def kernel(*refs):
        piece_refs = refs[:count]
        g_ref, u_ref, d_ref, gate_ref, up_ref, low_g_ref, low_u_ref = refs[count : count + 7]
        out_refs, (full, acc) = refs[count + 7 : 2 * count + 7], refs[2 * count + 7 :]
        step = pl.program_id(0)

        @pl.when(step == 0)
        def _():
            gather_rows(piece_refs, full)

        hidden_grad = product(full[...], d_ref[...])
        gate = gate_ref[...].astype(f32)
        _, back_glu = jax.vjp(glu_pair, gate, up_ref[...].astype(f32))
        gate_grad, up_grad = back_glu(hidden_grad)
        low_gate, low_up = gate_grad.astype(bf16), up_grad.astype(bf16)
        low_g_ref[...] = low_gate
        low_u_ref[...] = low_up
        part = against(low_gate, g_ref[...]) + against(low_up, u_ref[...])

        @pl.when(step == 0)
        def _():
            acc[...] = part

        @pl.when(step > 0)
        def _():
            acc[...] += part

        @pl.when(step == pl.num_programs(0) - 1)
        def _():
            for index, piece in enumerate(out_refs):
                piece[...] = acc[index * own : (index + 1) * own, :].astype(bf16)

    plane = lambda k: pl.BlockSpec((width, blk), lambda j: (0, k * (units // blk) + j))
    columns = pl.BlockSpec((tok, blk), lambda j: (0, j))
    result = pl.pallas_call(
        kernel,
        out_shape=[jax.ShapeDtypeStruct((tok, units), bf16)] * 2
        + [jax.ShapeDtypeStruct((own, width), bf16)] * count,
        grid=(units // blk,),
        in_specs=in_pieces_of(count, own, width)
        + [plane(0), plane(1), plane(2), columns, columns],
        out_specs=[columns] * 2
        + [pl.BlockSpec((own, width), lambda j: (0, 0))] * count,
        scratch_shapes=[pltpu.VMEM((tok, width), bf16), pltpu.VMEM((tok, width), f32)],
        compiler_params=pltpu.CompilerParams(vmem_limit_bytes=60 * MIB),
        cost_estimate=small_cost(6 * tok * width * units),
        name="feed_back",
    )(*pieces, w_ff, w_ff, w_ff, gate_raw, upward)
    return result[0], result[1], result[2:]


def column_grads(products, others, name, blk, every, parity, added=None):
    width = products[0][0][0].shape[1]
    operands, specs = [], []
    for left, right in products:
        operands += [*left, right]
        specs += [
            pl.BlockSpec((piece.shape[0], blk), lambda i, par: (0, every * i + par[0]))
            for piece in left
        ]
        specs.append(whole(right.shape))
    operands += others
    specs += [
        pl.BlockSpec((blk, other.shape[1]), lambda i, par: (every * i + par[0], 0))
        for other in others
    ]
    total = sum(mat.shape[1] for _, mat in products) + sum(other.shape[1] for other in others)
    counts = [len(left) for left, _ in products]
    out_spec = pl.BlockSpec((blk, total), lambda i, par: (i, 0))
    if added is not None:
        operands.append(added)
        specs.append(out_spec)

    def kernel(par_ref, *refs):
        o_ref, refs = refs[-1], list(refs[:-1])
        a_ref = refs.pop() if added is not None else None

        def give(value, place):
            columns = slice(place, place + value.shape[1])
            if a_ref is not None:
                value = value.astype(f32) + a_ref[:, columns].astype(f32)
            o_ref[:, columns] = value.astype(bf16)
            return columns.stop

        place = 0
        for count in counts:
            rows = jnp.concatenate([ref[...] for ref in refs[:count]], axis=0)
            place = give(across(rows, refs[count][...]), place)
            refs = refs[count + 1 :]
        for ref in refs:
            place = give(ref[...], place)

    return pl.pallas_call(
        kernel,
        out_shape=jax.ShapeDtypeStruct((width // every, total), bf16),
        grid_spec=pltpu.PrefetchScalarGridSpec(
            num_scalar_prefetch=1,
            grid=(width // blk // every,),
            in_specs=specs,
            out_specs=out_spec,
        ),
        compiler_params=pltpu.CompilerParams(vmem_limit_bytes=60 * MIB),
        cost_estimate=small_cost(1024),
        name=name,
    )(parity.reshape(1), *operands)


def crossed(piece, axis, bit):
    length = lax.axis_size(axis)
    return lax.ppermute(piece, axis, [(i, i ^ bit) for i in range(length)])


def spread_start(piece, axis):
    held = {0: piece}
    bit = lax.axis_size(axis) // 2
    while bit:
        held.update({k | bit: crossed(held[k], axis, bit) for k in list(held)})
        bit //= 2
    return [held[k] for k in range(1, len(held))]


def fold_start(chunks, axis):
    terms = {k: [chunk] for k, chunk in enumerate(chunks)}
    bit = 1
    while bit < len(chunks):
        for k in [k for k in terms if k & bit]:
            going = terms.pop(k)
            going = going[0] if len(going) == 1 else summed(going).astype(bf16)
            terms[k ^ bit].append(crossed(going, axis, bit))
        bit *= 2
    return terms[0]


def folded(chunks, axis):
    return summed(fold_start(chunks, axis))


def with_work(arrived, work):
    return lax.optimization_barrier((arrived, work))


def passed_along(shard, axis, by):
    length = lax.axis_size(axis)
    pairs = [(i, i + by) for i in range(length) if 0 <= i + by < length]
    return lax.ppermute(shard, axis, pairs)


def summed(terms):
    total = terms[0].astype(f32)
    for term in terms[1:]:
        total = total + term.astype(f32)
    return total


def rank_among(keys_own):
    count = keys_own.shape[0]
    place = jnp.arange(count, dtype=jnp.int32)
    same = (keys_own[None, :] == keys_own[:, None]) & (place[None, :] < place[:, None])
    return jnp.sum(same.astype(jnp.int32), axis=1)


def plan(lengths, order, micro, block_rows):
    devices = lax.axis_size("dp")
    parts = lax.axis_size("tensor")
    me = lax.axis_index("dp")
    part = lax.axis_index("tensor")
    tok = micro * block_rows
    own = tok // parts
    stretch = devices * block_rows
    seqs = lengths.shape[0]
    given_len = jnp.take(lengths, order)
    given_start = jnp.cumsum(given_len) - given_len
    dealt_start = jnp.cumsum(lengths) - lengths
    seq_ids = jnp.arange(seqs, dtype=jnp.int32)
    shift_given = jnp.take(dealt_start, order) - given_start
    pieces = tok // LMIN + 2
    runs = tok // stretch + 1
    per_piece = block_rows * (-(-tok // stretch)) + (parts - 1) * runs
    capacity = -(-(pieces * (per_piece // parts) + 1) // 8) * 8
    kept = -(-(tok // parts + seqs + 1) // 8) * 8

    def pick(table, index):
        return jnp.sum(jnp.where(index[:, None] == seq_ids[None, :], table[None, :], 0), axis=1)

    local = jnp.arange(tok, dtype=jnp.int32)
    stream = local // block_rows * stretch + me * block_rows + local % block_rows
    arrival = jnp.sum((stream[:, None] >= given_start[None, 1:]).astype(jnp.int32), axis=1)
    dealt = stream + pick(shift_given, arrival)
    target = dealt // tok
    quarter = dealt % parts
    send_slot = target * capacity + rank_among(target * parts + quarter)
    send_slot = jnp.where(quarter == part, send_slot, -1)
    keep_rank = rank_among(quarter)
    keep_slot = (part ^ quarter) * kept + keep_rank

    place = me * tok + jnp.arange(own, dtype=jnp.int32) * parts + part
    own_seq = jnp.sum((place[:, None] >= dealt_start[None, 1:]).astype(jnp.int32), axis=1)
    shift_dealt = jnp.sum(
        jnp.where(order[None, :] == seq_ids[:, None], -shift_given[None, :], 0), axis=1
    )
    anchor = place + pick(shift_dealt, own_seq)
    source = anchor % stretch // block_rows
    prior = (anchor[None, :] < anchor[:, None]) & (source[None, :] == source[:, None])
    recv_slot = source * capacity + jnp.sum(prior.astype(jnp.int32), axis=1)

    total = devices * capacity
    slots = jnp.arange(total, dtype=jnp.int32)
    sender = (slots[:, None] == send_slot[None, :]).astype(bf16)
    receiver = (recv_slot[:, None] == slots[None, :]).astype(bf16)
    mine = jnp.where(quarter == part, keep_rank, -1)
    chosen = (jnp.arange(kept, dtype=jnp.int32)[:, None] == mine[None, :]).astype(bf16)
    compact = against(chosen, sender, bf16)
    homing = (
        keep_slot[:, None] == jnp.arange(parts * kept, dtype=jnp.int32)[None, :]
    ).astype(bf16)

    held = part ^ jnp.arange(parts, dtype=jnp.int32)
    rows = (jnp.arange(own, dtype=jnp.int32)[None, :] * parts + held[:, None]).reshape(tok)
    both = me * tok + jnp.concatenate([rows - tok, rows])
    ext_seq = jnp.sum((both[:, None] >= dealt_start[None, 1:]).astype(jnp.int32), axis=1)
    start = pick(dealt_start, ext_seq[tok:])
    high_bound = both[tok:]
    low_bound = jnp.maximum(start, high_bound - (WIN - 1))
    return sender, receiver, compact, homing, (low_bound, high_bound, both), high_bound - start


def body(
    hidden_in,
    layer_inputs,
    out_grad,
    lengths,
    order,
    w_query,
    w_keyval,
    w_out,
    w_left,
    w_right,
    w_gateup,
    w_down,
    w_pergate,
    w_perproj,
    gains,
    head_gains,
):
    devices = lax.axis_size("dp")
    me = lax.axis_index("dp")
    parts = lax.axis_size("tensor")
    part = lax.axis_index("tensor")
    micro, block_rows, width = hidden_in.shape
    per_width = layer_inputs.shape[2]
    tok = micro * block_rows
    assert tok == WIN
    sender, receiver, compact, homing, bounds, own_pos = plan(lengths, order, micro, block_rows)

    kv_cols = part // (parts // KVH) * HD
    kv_own = lax.dynamic_slice_in_dim(w_keyval, kv_cols, HD, 2)
    gains_high = lax.reduce_precision(gains, 8, 7)
    gains_low = (gains - gains_high).astype(bf16)
    gain_cols = jnp.concatenate([gains_high.astype(bf16), gains_low], axis=0)
    gain_cols = jnp.pad(gain_cols, ((0, LANES - gain_cols.shape[0]), (0, 0))).T
    q_width = w_query.shape[1]
    rank = w_left.shape[1]

    def gather_columns(pieces):
        marks = [0]
        for piece in pieces:
            marks.append(marks[-1] + piece.shape[1])
        full = lax.all_gather(jnp.concatenate(pieces, axis=1), "dp", axis=0, tiled=True)
        return full, [full[:, a:b] for a, b in zip(marks[:-1], marks[1:])]

    first = [w_query, kv_own[0], kv_own[1], w_out.T, w_left, w_right.T, gain_cols]
    bundle_a, (wq, wk, wv, wo_t, wl, wr_t, gain_f) = gather_columns(first)
    units = w_down.shape[0]
    packed_in = product(sender, hidden_in.reshape(tok, width), bf16)
    come_in = lax.all_to_all(packed_in, "dp", 0, 0, tiled=True)
    low_inputs = product(receiver, come_in, bf16)
    inputs = low_inputs.astype(f32)
    token_pieces = spread_start(low_inputs, "tensor")
    w_ff, _ = gather_columns([w_gateup[0], w_gateup[1], w_down.T])
    w_gains = gain_f.T
    gains_f = w_gains[:6].astype(f32) + w_gains[6:12].astype(f32)
    angles = own_pos.astype(f32)[:, None] * frequencies()

    def homeward(rows_own):
        return lax.all_to_all(across(receiver, rows_own, bf16), "dp", 0, 0, tiled=True)

    block = width // devices
    paired = devices > 1 and block % (2 * LANES) == 0
    low_bit = me % 2
    groups = [list(range(k, devices, 2)) for k in range(2)] if paired else None

    def scattered(grads):
        return lax.psum_scatter(
            grads, "dp", scatter_dimension=0, axis_index_groups=groups, tiled=True
        )

    def grads_leaving(make):
        return make(block, 2, 1 - low_bit) if paired else make(2 * LANES, 1, me * 0)

    def beside_first(chunks, work):
        chunks = list(chunks)
        chunks[-2], work = with_work(chunks[-2], work)
        return chunks, work

    def grads_come(leaving):
        return crossed(leaving, "dp", 1) if paired else leaving

    def grads_staying(make, come):
        return make(block, 2, low_bit, come) if paired else come

    cosine, sine = jnp.cos(angles), jnp.sin(angles)
    heads = q_width // HD
    all_in, raw, queries, own_kv = project(
        [low_inputs] + token_pieces, gains_f[:1], bundle_a, head_gains, cosine, sine, heads
    )
    normal_in = normed(inputs, gains_f[0])
    low_in = normal_in.astype(bf16)
    tails = passed_along(own_kv, "dp", 1)
    low_att, branch_parts = attend(queries, tails, own_kv, *bounds, bundle_a, parts)
    branch = folded(branch_parts, "tensor")

    low_rank = product(low_in, wl, bf16)
    laurel_raw = against(low_rank, wr_t)
    first_sum = (
        inputs + normed(branch, gains_f[1]) + normal_in + normed(laurel_raw, gains_f[2])
    ) * half_root
    low_mid = normed(first_sum, gains_f[3]).astype(bf16)

    all_mid = [low_mid] + spread_start(low_mid, "tensor")
    rest_in = jnp.concatenate(
        [layer_inputs.reshape(tok, per_width), out_grad.reshape(tok, width)], axis=1
    )
    third = [w_pergate, w_perproj.T]
    rest_out = product(sender, rest_in, bf16)
    (rest_out, third), w_ff = with_work((rest_out, third), w_ff)
    _, (wg, wp_t) = gather_columns(third)
    come_rest = lax.all_to_all(rest_out, "dp", 0, 0, tiled=True)
    gate_raw, upward, low_hidden, feed_parts = feed_forward(all_mid, w_ff, units)
    feed_parts, come_rest = with_work(feed_parts, come_rest)
    fed_pieces = fold_start(feed_parts, "tensor")
    rest = product(receiver, come_rest, bf16)
    layer_in = rest[:, :per_width].astype(f32)
    cotangent = rest[:, per_width:].astype(f32)
    feed_raw = summed(fed_pieces)

    second_sum = first_sum + normed(feed_raw, gains_f[4])
    low_second = second_sum.astype(bf16)
    pre_gate = product(low_second, wg)
    low_gated = (gelu_tanh(pre_gate) * layer_in).astype(bf16)
    per_raw = against(low_gated, wp_t)
    result = second_sum + normed(per_raw, gains_f[5])

    _, back_per = jax.vjp(normed, per_raw, gains_f[5])
    per_grad, grad_g5 = back_per(cotangent)
    low_per = per_grad.astype(bf16)
    gated_grad = product(low_per, wp_t)
    gelu_out, back_gelu = jax.vjp(gelu_tanh, pre_gate)
    low_pre = back_gelu(gated_grad * layer_in)[0].astype(bf16)
    layer_grad = gated_grad * gelu_out
    second_grad = cotangent + against(low_pre, wg)
    _, back_feed = jax.vjp(normed, feed_raw, gains_f[4])
    feed_grad, grad_g4 = back_feed(second_grad)
    low_feed = feed_grad.astype(bf16)

    feed_pieces = spread_start(low_feed, "tensor")
    grad_perproj = across(low_per, low_gated, bf16)
    grad_pergate = across(low_second, low_pre, bf16)
    low_result = jnp.concatenate([result.astype(bf16), layer_grad.astype(bf16)], axis=1)
    come_one = homeward(low_result)
    feed_pieces, (grad_perproj, grad_pergate, come_one) = with_work(
        feed_pieces, (grad_perproj, grad_pergate, come_one)
    )
    all_feed = [low_feed] + feed_pieces

    home_one = product(compact, come_one, bf16)
    home_pieces = spread_start(home_one, "tensor")
    low_gate, low_up, mid_parts = feed_back(all_feed, w_ff, gate_raw, upward)
    mid_parts, home_pieces[0] = with_work(mid_parts, home_pieces[0])
    mid_parts, home_pieces[1] = with_work(mid_parts, home_pieces[1])

    def ff_grads_of(*where):
        return column_grads(
            [(all_mid, low_gate), (all_mid, low_up), (all_feed, low_hidden)],
            [grad_pergate, grad_perproj],
            "feed_grads",
            *where,
        )

    mid_parts, ff_leaving = beside_first(mid_parts, grads_leaving(ff_grads_of))
    mid_pieces = fold_start(mid_parts, "tensor")
    ff_grads = grads_staying(ff_grads_of, grads_come(ff_leaving))
    mid_pieces, ff_grads = with_work(mid_pieces, ff_grads)
    s_ff = scattered(ff_grads)
    mid_grad = summed(mid_pieces)

    _, back_mid = jax.vjp(normed, first_sum, gains_f[3])
    first_part, grad_g3 = back_mid(mid_grad)
    shared = (second_grad + first_part) * half_root
    _, back_laurel = jax.vjp(normed, laurel_raw, gains_f[2])
    laurel_grad, grad_g2 = back_laurel(shared)
    low_laurel = laurel_grad.astype(bf16)
    _, back_branch = jax.vjp(normed, branch, gains_f[1])
    branch_grad, grad_g1 = back_branch(shared)
    low_branch = branch_grad.astype(bf16)

    branch_pieces = spread_start(low_branch, "tensor")
    low_rank_grad = product(low_laurel, wr_t, bf16)
    grad_right = across(low_laurel, low_rank, bf16)
    grad_left = across(low_in, low_rank_grad, bf16)
    small = jnp.concatenate([grad_left, grad_right], axis=1)
    gain_part = jnp.stack([grad_g1, grad_g2, grad_g3, grad_g4, grad_g5])
    branch_pieces, (small, gain_part) = with_work(branch_pieces, (small, gain_part))
    all_branch = [low_branch] + branch_pieces

    query_grad, own_grad, halo_grad = attend_back(
        queries, tails, own_kv, all_branch, *bounds, bundle_a
    )
    query_grad, home_pieces[-1] = with_work(query_grad, home_pieces[-1])
    next_grad = passed_along(halo_grad, "dp", -1)
    low_qkv, head_grads, in_parts = project_back(
        query_grad, own_grad, next_grad, raw, head_gains, cosine, sine, bundle_a, parts
    )

    head_cols = head_grads.reshape(-1, width // devices)
    head_count = head_cols.shape[0]
    head_cols = jnp.tile(head_cols, (1, devices))
    last_cols = jnp.concatenate([gain_part, head_cols], axis=0).astype(bf16)
    last_cols = jnp.pad(last_cols, ((0, LANES - last_cols.shape[0]), (0, 0))).T
    def at_grads_of(*where):
        return column_grads(
            [([all_in], low_qkv), (all_branch, low_att)],
            [small, last_cols],
            "attention_grads",
            *where,
        )

    in_pieces = fold_start(in_parts, "tensor")
    at_leaving = grads_leaving(at_grads_of)
    in_pieces, at_leaving = with_work(in_pieces, at_leaving)
    in_attn = summed(in_pieces)
    normal_grad = in_attn + against(low_rank_grad, wl) + shared
    _, back_in = jax.vjp(normed, inputs, gains_f[0])
    in_part, grad_g0 = back_in(normal_grad)
    input_grad = shared + in_part
    extra = jnp.pad(
        grad_g0.reshape(devices, 1, block),
        ((0, 0), (receiver.shape[1] // devices - 1, 0), (0, width - block)),
    )
    sent_two = across(receiver, input_grad.astype(bf16)) + extra.reshape(-1, width)
    come_two = lax.all_to_all(sent_two.astype(bf16), "dp", 0, 0, tiled=True)
    early = s_ff[:, 3 * units :]
    bit = 1
    while bit < parts:
        early = summed([early, crossed(early, "tensor", bit)])
        early = early.astype(bf16) if 2 * bit < parts else early
        bit *= 2
    at_grads = grads_staying(at_grads_of, grads_come(at_leaving))
    at_grads, (s_ff, come_two) = with_work(at_grads, (s_ff, come_two))
    s_at = scattered(at_grads)
    come_two, early = with_work(come_two, early)
    g0_part = jnp.sum(come_two.reshape(devices, -1, width)[:, -1, :block].astype(f32), axis=0)
    home_two = product(compact, come_two) + jnp.pad(
        g0_part[None], ((compact.shape[0] - 1, 0), (0, width - block))
    )
    o_kv = q_width + 2 * HD
    o_small = o_kv + w_out.shape[0]
    kv_cols = 2 * HD
    exchanged = jnp.concatenate([s_at[:, q_width:o_kv], s_at[:, o_small:]], axis=1)
    bit = 1
    while bit < parts // KVH:
        exchanged = summed([exchanged, crossed(exchanged, "tensor", bit)]).astype(bf16)
        bit *= 2
    home_two = home_two.astype(bf16)
    two_pieces, exchanged = with_work(spread_start(home_two, "tensor"), exchanged)
    all_two = jnp.concatenate([home_two] + two_pieces, axis=0)
    back_two = product(homing, all_two, bf16)
    g0_terms = all_two.reshape(parts, -1, width)[:, -1, :block].astype(f32)
    while g0_terms.shape[0] > 1:
        middle = g0_terms.shape[0] // 2
        g0_terms = g0_terms[:middle] + g0_terms[middle:]

    shard_gateup = jnp.stack([s_ff[:, :units], s_ff[:, units : 2 * units]]).astype(f32)
    shard_down = s_ff[:, 2 * units : 3 * units].T.astype(f32)
    shard_query = s_at[:, :q_width].astype(f32)
    shard_out = s_at[:, o_kv:o_small].T.astype(f32)
    arrived = crossed(exchanged, "tensor", bit)
    kv_sum, kv_other = exchanged[:, :kv_cols], arrived[:, :kv_cols]
    small_sum = summed([exchanged[:, kv_cols:], arrived[:, kv_cols:]])
    shard_left = small_sum[:, :rank]
    shard_right = small_sum[:, rank : 2 * rank].T
    shard_pergate = early[:, :per_width]
    shard_perproj = early[:, per_width:].T
    last_sum = small_sum[:, 2 * rank :].T
    shard_gains = jnp.concatenate([g0_terms, last_sum[:5]], axis=0)
    head_total = last_sum[5 : 5 + head_count].reshape(2, HD)
    upper = part // (parts // KVH) == 1
    low_head = jnp.where(upper, kv_other, kv_sum).astype(f32)
    high_head = jnp.where(upper, kv_sum, kv_other).astype(f32)
    shard_keyval = jnp.stack(
        [
            jnp.concatenate([low_head[:, :HD], high_head[:, :HD]], axis=1),
            jnp.concatenate([low_head[:, HD:], high_head[:, HD:]], axis=1),
        ]
    )
    back_one = product(homing, jnp.concatenate([home_one] + home_pieces, axis=0), bf16)
    return (
        back_one[:, :width].reshape(micro, block_rows, width),
        back_two.reshape(micro, block_rows, width),
        back_one[:, width:].reshape(micro, block_rows, per_width),
        shard_query,
        shard_keyval,
        shard_out,
        shard_left,
        shard_right,
        shard_gateup,
        shard_down,
        shard_pergate,
        shard_perproj,
        shard_gains,
        head_total,
    )


def solution(mesh):
    placed = (
        P(None, "dp", None),
        P(None, "dp", None),
        P(None, "dp", None),
        P(),
        P(),
        P("dp", "tensor"),
        P(None, "dp", None),
        P("tensor", "dp"),
        P("dp", None),
        P(None, "dp"),
        P(None, "dp", "tensor"),
        P("tensor", "dp"),
        P("dp", None),
        P(None, "dp"),
        P(None, "dp"),
        P(),
    )
    return jax.shard_map(
        body,
        mesh=mesh,
        in_specs=placed,
        out_specs=(
            P(None, "dp", None),
            P(None, "dp", None),
            P(None, "dp", None),
            P("dp", "tensor"),
            P(None, "dp", None),
            P("tensor", "dp"),
            P("dp", None),
            P(None, "dp"),
            P(None, "dp", "tensor"),
            P("tensor", "dp"),
            P("dp", None),
            P(None, "dp"),
            P(None, "dp"),
            P(),
        ),
        check_vma=False,
    )
```
